32 devices in a mesh: rows: 8 (over y, x, core), loop: 4 (over z).
Axes of the slice: x: 2, y: 2, z: 4, core: 2. Of those that a mesh axis runs over, the one named last changes fastest.
Arguments:
- integrals: float32 [2, 2, 8192, 8192], P(None, None, 'rows', 'loop'), may hold values from -6 to 6
- mask: int32 [2, 64, 64], P(None, 'rows', 'loop'), may hold values 0 or 1
- coeffs: float32 [8192, 640], P('loop'), may hold values from -0.0625 to 0.0625
Outputs:
- exchange: float32 [8192, 8192], P('rows', 'loop')
The draws below stay inside these ranges and needn't reach their ends.
All inputs are finite; a program needn't handle non-finite values. No bound on the sum of `mask` on one device may be relied on, other than what follows from the above.
Results may differ from the reference program's by a relative error of at most 0.00009.
Values sent between devices are 32-bit elements; how exact they have to be, the bound alone decides.
A program may use at most 192 MiB of HBM per device.

```python
import jax
import jax.numpy as jnp
from jax import lax

NBF = 8192
NOCC = 640
TILE = 128
NSLAB = 2
AUX = 2


def plant(result, key, smallest, largest):
    index_at = [jax.random.randint(jax.random.fold_in(key, axis), (), 0, length) for axis, length in enumerate(result.shape)]
    longest = result.shape.index(max(result.shape))
    next_to = index_at[:longest] + [(index_at[longest] + 1) % result.shape[longest]] + index_at[longest + 1:]
    return result.at[tuple(index_at)].set(smallest).at[tuple(next_to)].set(largest)


def shard_levels(own_key, shape, split, low, largest):
    gain, own = 1.0, jax.random.fold_in(own_key, 6)
    for dim, blocks in split:
        draws = jnp.exp(jax.random.uniform(jax.random.fold_in(own, dim), (blocks,), jnp.float32, low / len(split), largest / len(split)))
        gain = gain * jnp.repeat(draws, shape[dim] // blocks).reshape([-1 if axis == dim else 1 for axis in range(len(shape))])
    return gain


def normal_values(key, extent, width, most, split=(), dtype=jnp.bfloat16):
    result = jax.random.normal(key, extent, jnp.float32) * width
    if len(split) > 0:
        result = shard_levels(key, extent, split, -0.22, 0.18) * result
    return jnp.clip(result, min=-most, max=most).astype(dtype)


def setup_inputs(seed: int = 0) -> dict:
    arg_keys = jax.random.split(jax.random.key(seed), 4)
    integrals = normal_values(arg_keys[0], (NSLAB, AUX, NBF, NBF), 1.0, 6.0, ((2, 8), (3, 4)), jnp.float32)
    mask = plant((jax.random.randint(arg_keys[1], (NSLAB, NBF // TILE, NBF // TILE), 0, 2) < 1).astype(jnp.int32), jax.random.fold_in(arg_keys[1], 1), 0, 1)
    coeffs = normal_values(arg_keys[2], (NBF, NOCC), NBF ** -0.5, 0.0625, ((0, 4),), jnp.float32)
    return {"integrals": integrals, "mask": mask, "coeffs": coeffs}


def reference(integrals, mask, coeffs):
    blocks = mask.astype(jnp.float32)[:, None, :, None, :, None]
    shaped = integrals.reshape(NSLAB, AUX, NBF // TILE, TILE, NBF // TILE, TILE)
    masked = (shaped * blocks).reshape(NSLAB * AUX, NBF, NBF)
    half = jnp.einsum('pml,li->ipm', masked, coeffs, precision=lax.Precision.HIGHEST)
    scale = 1.0 / jnp.sqrt(jnp.float32(NSLAB * AUX * NOCC))
    total = jnp.einsum('ipm,ipn->mn', half, half, precision=lax.Precision.HIGHEST)
    return (total * scale).astype(jnp.float32)
```

```python
import functools

import jax
import jax.numpy as jnp
from jax import lax
from jax.experimental import pallas as pl
from jax.experimental.pallas import tpu as pltpu
from jax.sharding import PartitionSpec as P

TILE = 128
WIDE = 2 * TILE
CHUNK = 64
SPAN = 256
DEEP = 512
HOP = 3
REACH = 2
SLOTS = 8
BUFFERS = 4
LOAD = 256
MESH = pl.DeviceIdType.MESH


def split(x):
    high = x.astype(jnp.bfloat16)
    low = (x - high.astype(jnp.float32)).astype(jnp.bfloat16)
    return high, low


def ring_place(pair, pairs):
    if pairs == 4:
        return pair + (pair // 2) * (1 - 2 * lax.rem(pair, 2))
    return pair


def place_of(part, tile, block, parts, tiles, norbit):
    inner = tile * norbit + block * TILE
    last = block * (tiles * TILE) + tile * TILE
    if isinstance(part, int):
        return part * tiles * norbit + (inner if part < parts - 1 else last)
    return part * (tiles * norbit) + jnp.where(part < parts - 1, inner, last)


def plan(parts, tiles, norbit, lag, last_done):
    groups, blocks = parts * norbit // SPAN, norbit // TILE
    starts, free = [], 0
    for g in range(groups - 1):
        last = max(
            place_of(h // blocks, tiles - 1, h % blocks, parts, tiles, norbit) + TILE - 1 for h in (2 * g, 2 * g + 1)
        )
        starts.append(max(last // CHUNK + lag, free))
        free = starts[-1] + 1 + 2 * tiles
    return starts + [max(last_done, free)]


def exchange_kernel(
    loops, row_count, integrals_ref, mask_ref, coeffs_ref, acc_ref, left_ref, right_ref,
    own, pin, sin, cols, high_ref, low_ref, tile, room, tile_sem, room_sem,
    up_send, up_recv, dn_send, dn_recv, ch_send, ch_recv, pt_send, pt_recv,
):
    nslab, naux, mrows, lcols = integrals_ref.shape
    norbit = coeffs_ref.shape[1]
    parts = nslab * naux
    tiles = mrows // WIDE
    blocks = norbit // TILE
    tile_count = parts * tiles
    deep = tile.shape[2]
    cuts = lcols // deep
    count = own.shape[0] // CHUNK
    ring = pin.shape[0] // CHUNK
    pairs = row_count // 2
    r, l = lax.axis_index("rows"), lax.axis_index("loop")
    pair, core = r // 2, lax.rem(r, 2)
    partner = r + 1 - 2 * core
    turn = 1 - 2 * core
    place = ring_place(pair, pairs)
    far = lax.rem((place - ring_place(l, pairs)) * turn + pairs, pairs)
    ahead = ring_place(lax.rem(place + turn + pairs, pairs), pairs) * 2 + core
    behind = ring_place(lax.rem(place - turn + pairs, pairs), pairs) * 2 + core

    def deep_of(q):
        return pl.ds(pl.multiple_of(q * deep, deep), deep)

    def row_of(part, m, block):
        return pl.ds(pl.multiple_of(place_of(part, m, block, parts, tiles, norbit), TILE), TILE)

    def fetch(u, q):
        part, m = u // tiles, lax.rem(u, tiles)
        slot = lax.rem(u * cuts + q, BUFFERS)
        return pltpu.make_async_copy(
            integrals_ref.at[
                part // naux, lax.rem(part, naux), pl.ds(pl.multiple_of(m * WIDE, WIDE), WIDE), deep_of(q)
            ],
            tile.at[slot],
            tile_sem.at[slot],
        )

    def fetch_next(u, q):
        i = u * cuts + q + BUFFERS

        @pl.when(i < tile_count * cuts)
        def _():
            fetch(i // cuts, lax.rem(i, cuts)).start()

    def load(n):
        slot = lax.rem(n, 2)
        at = pl.ds(pl.multiple_of(n * LOAD, LOAD), LOAD)
        return pltpu.make_async_copy(coeffs_ref.at[at, :], room.at[slot], room_sem.at[slot])

    def half(u, q):
        part, m = u // tiles, lax.rem(u, tiles)
        slab = part // naux
        fetch(u, q).wait()

        @pl.when(q == 0)
        def _():
            for b in range(blocks):
                own[row_of(part, m, b), :] = jnp.zeros((TILE, WIDE), jnp.float32)

        def piece(i, j):
            keep = mask_ref[slab, m * (WIDE // TILE) + i, q * (deep // TILE) + j].astype(jnp.float32)
            return tile[lax.rem(u * cuts + q, BUFFERS), i * TILE : (i + 1) * TILE, j * TILE : (j + 1) * TILE] * keep

        held = jnp.concatenate(
            [jnp.concatenate([piece(i, j) for j in range(deep // TILE)], axis=1) for i in range(WIDE // TILE)], axis=0
        )
        high, low = split(held)

        def times(a, b):
            return lax.dot_general(a, b, (((1,), (1,)), ((), ())), preferred_element_type=jnp.float32)

        at = deep_of(q)
        value = times(high_ref[:, at], high) + times(high_ref[:, at], low) + times(low_ref[:, at], high)
        for b in range(blocks):
            rows = row_of(part, m, b)
            own[rows, :] = own[rows, :] + value[b * TILE : (b + 1) * TILE]

        fetch_next(u, q)

    for n in range(2):
        load(n).start()
    for i in range(BUFFERS):
        fetch(i // cuts, i % cuts).start()

    barrier = pltpu.get_barrier_semaphore()
    for other in (partner, ahead, behind):
        pl.semaphore_signal(barrier, inc=1, device_id={"rows": other}, device_id_type=MESH)

    @pl.when(l > 0)
    def _():
        pl.semaphore_signal(barrier, inc=1, device_id={"loop": l - 1}, device_id_type=MESH)

    @pl.when(l < loops - 1)
    def _():
        pl.semaphore_signal(barrier, inc=1, device_id={"loop": l + 1}, device_id_type=MESH)

    @pl.loop(0, cuts)
    def _(q):
        for k in range(deep // LOAD):
            n = q * (deep // LOAD) + k
            load(n).wait()
            at = pl.ds(pl.multiple_of(n * LOAD, LOAD), LOAD)
            high_ref[:, at], low_ref[:, at] = split(room[lax.rem(n, 2)].T)

            @pl.when(n + 2 < lcols // LOAD)
            def _():
                load(n + 2).start()

        half(0, q)

    neighbours = jnp.where(l > 0, 1, 0) + jnp.where(l < loops - 1, 1, 0)
    pl.semaphore_wait(barrier, 3 + neighbours)

    def rows_of(j):
        return pl.ds(pl.multiple_of(j * CHUNK, CHUNK), CHUNK)

    def slot_of(j):
        return pl.ds(pl.multiple_of(lax.rem(j, ring) * CHUNK, CHUNK), CHUNK)

    def copy(src, dst, send, recv, j, target):
        return pltpu.make_async_remote_copy(
            src_ref=src, dst_ref=dst, send_sem=send.at[lax.rem(j, SLOTS)], recv_sem=recv.at[j],
            device_id=target, device_id_type=MESH,
        )

    def up(j):
        return copy(pin.at[slot_of(j)], pin.at[slot_of(j)], up_send, up_recv, j, {"loop": l + 1})

    def down(j):
        return copy(sin.at[slot_of(j)], sin.at[slot_of(j)], dn_send, dn_recv, j, {"loop": l - 1})

    def chain(j):
        ref = cols.at[core, rows_of(j)]
        return copy(ref, ref, ch_send, ch_recv, j, {"rows": ahead})

    def share(j):
        ref = cols.at[core, rows_of(j)]
        return copy(ref, ref, pt_send, pt_recv, j, {"rows": partner})

    def taken(j):
        ref = cols.at[1 - core, rows_of(j)]
        return copy(ref, ref, pt_send, pt_recv, j, {"rows": partner})

    def send(make, j):
        @pl.when(j >= SLOTS)
        def _():
            make(j - SLOTS).wait_send()

        make(j).start()

    def line(held, make, j, first, last):
        @pl.when((j >= 0) & (j < count))
        def _():
            at, slot = rows_of(j), slot_of(j)

            @pl.when(first)
            def _():
                held[slot, :] = own[at, :]

            @pl.when(jnp.logical_not(first))
            def _():
                make(j).wait_recv()
                held[slot, :] = held[slot, :] + own[at, :]

            @pl.when(jnp.logical_not(last))
            def _():
                send(make, j)

    settle = HOP * jnp.maximum(l, loops - 1 - l)
    lag = HOP * (loops - 1) + REACH * pairs
    starts = plan(parts, tiles, norbit, lag, count - 1 + HOP * (loops - 1))
    groups = len(starts)
    total_steps = max(count + lag, starts[-1] + 1)
    final = count - 2 * TILE * tiles // CHUNK

    def multiply(g, n):
        @pl.when(n == 0)
        def _():
            @pl.loop(0, tiles)
            def _(m):
                mine = pl.ds(pl.multiple_of(m * WIDE, WIDE), WIDE)
                for h in range(2):
                    block = 2 * g + h
                    high, low = split(own[row_of(block // blocks, m, lax.rem(block, blocks)), :].T)
                    left_ref[mine, h * TILE : (h + 1) * TILE] = high
                    left_ref[mine, SPAN + h * TILE : SPAN + (h + 1) * TILE] = high
                    left_ref[mine, 2 * SPAN + h * TILE : 2 * SPAN + (h + 1) * TILE] = low

        @pl.when(n > 0)
        def _():
            held, m = (n - 1) // tiles, lax.rem(n - 1, tiles)
            both = []
            for h in range(2):
                block = 2 * g + h
                both.append(cols[held, row_of(block // blocks, m, lax.rem(block, blocks)), :])
            high, low = split(jnp.concatenate(both, axis=0))
            right = jnp.concatenate([high, low, high], axis=0)
            theirs = pl.ds(pl.multiple_of((n - 1) * WIDE, WIDE), WIDE)

            @pl.when(g == 0)
            def _():
                acc_ref[:, theirs] = jnp.zeros((mrows, WIDE), jnp.float32)

            acc_ref[:, theirs] = acc_ref[:, theirs] + jnp.dot(left_ref[...], right, preferred_element_type=jnp.float32)

    def step(t, carry):
        line(pin, up, t - HOP * l, l == 0, l == loops - 1)
        line(sin, down, t - HOP * (loops - 1 - l), l == loops - 1, l == 0)

        done = t - settle

        @pl.when((done >= 0) & (done < count))
        def _():
            at, slot = rows_of(done), slot_of(done)
            total = pin[slot, :] + (sin[slot, :] - own[at, :])
            own[at, :] = total

            @pl.when(far == 0)
            def _():
                cols[core, at, :] = total

        passed = done - REACH * far

        @pl.when((passed >= 0) & (passed < count))
        def _():
            @pl.when(far > 0)
            def _():
                chain(passed).wait_recv()

            @pl.when(far < pairs - 1)
            def _():
                send(chain, passed)

            send(share, passed)

        ready = done - REACH * pairs

        @pl.when((ready >= 0) & (ready < count))
        def _():
            taken(ready).wait_recv()

        @pl.when((ready >= final) & (ready < count))
        def _():
            off = (ready - final) * CHUNK
            k = off // (tiles * TILE) * TILE + lax.rem(off, TILE)
            m = lax.rem(off // TILE, tiles)
            for held in range(2):
                high, low = split(cols[held, rows_of(ready), :])
                theirs = pl.ds(pl.multiple_of(held * mrows + m * WIDE, WIDE), WIDE)
                right_ref[pl.ds(pl.multiple_of(k, CHUNK), CHUNK), theirs] = high
                right_ref[pl.ds(pl.multiple_of(SPAN + k, CHUNK), CHUNK), theirs] = low

        g, begin = -1, 0
        for k, at in enumerate(starts):
            g = g + jnp.where(t >= at, 1, 0)
            begin = begin + jnp.where(t >= at, at - (starts[k - 1] if k else 0), 0)

        @pl.when((g >= 0) & (t - begin <= jnp.where(g < groups - 1, 2 * tiles, 0)))
        def _():
            multiply(g, t - begin)

        later, q = 1 + t // (cuts + 1), lax.rem(t, cuts + 1)

        @pl.when((later < tile_count) & (q < cuts))
        def _():
            half(later, q)

        return carry

    lax.fori_loop(0, total_steps, step, 0)

    def drain(i, carry):
        j = count - SLOTS + i

        @pl.when(l < loops - 1)
        def _():
            up(j).wait_send()

        @pl.when(l > 0)
        def _():
            down(j).wait_send()

        @pl.when(far < pairs - 1)
        def _():
            chain(j).wait_send()

        share(j).wait_send()
        return carry

    lax.fori_loop(0, SLOTS, drain, 0)


def finish_kernel(scale, acc_ref, left_ref, right_ref, out_ref):
    right = jnp.concatenate([right_ref[...], right_ref[:SPAN, :]], axis=0)
    value = acc_ref[...] + jnp.dot(left_ref[...], right, preferred_element_type=jnp.float32)
    out_ref[...] = value * scale


def local(loops, row_count, integrals, mask, coeffs):
    nslab, naux, mrows, lcols = integrals.shape
    norbit = coeffs.shape[1]
    depth = nslab * naux * norbit
    tiles = mrows // WIDE
    count = depth * tiles * WIDE // (CHUNK * WIDE)
    assert lcols == 2 * mrows and row_count == 2 * loops and mrows % WIDE == 0
    assert norbit % TILE == 0 and norbit >= SPAN and depth % SPAN == 0
    deep = min(DEEP, lcols)
    cuts = lcols // deep
    assert cuts + 1 <= norbit // CHUNK and nslab * naux * tiles * cuts >= BUFFERS and lcols >= 2 * LOAD
    ring = min(count, max(SLOTS + 2 * HOP, HOP * (loops + 1)) + 4)
    dma = pltpu.SemaphoreType.DMA
    vmem = pl.BlockSpec(memory_space=pltpu.VMEM)
    partial = pl.pallas_call(
        functools.partial(exchange_kernel, loops, row_count),
        out_shape=[
            jax.ShapeDtypeStruct((mrows, lcols), jnp.float32),
            jax.ShapeDtypeStruct((mrows, 3 * SPAN), jnp.bfloat16),
            jax.ShapeDtypeStruct((2 * SPAN, lcols), jnp.bfloat16),
        ],
        in_specs=[
            pl.BlockSpec(memory_space=pltpu.MemorySpace.HBM),
            pl.BlockSpec(memory_space=pltpu.SMEM),
            pl.BlockSpec(memory_space=pltpu.MemorySpace.HBM),
        ],
        out_specs=[vmem] * 3,
        scratch_shapes=[
            pltpu.VMEM((depth * tiles, WIDE), jnp.float32),
            pltpu.VMEM((ring * CHUNK, WIDE), jnp.float32),
            pltpu.VMEM((ring * CHUNK, WIDE), jnp.float32),
            pltpu.VMEM((2, depth * tiles, WIDE), jnp.float32),
            pltpu.VMEM((norbit, lcols), jnp.bfloat16),
            pltpu.VMEM((norbit, lcols), jnp.bfloat16),
            pltpu.VMEM((BUFFERS, WIDE, deep), jnp.float32),
            pltpu.VMEM((2, LOAD, norbit), jnp.float32),
            dma((BUFFERS,)),
            dma((2,)),
        ]
        + [dma((SLOTS,)), dma((count,))] * 4,
        compiler_params=pltpu.CompilerParams(
            collective_id=0, has_side_effects=True, vmem_limit_bytes=42 << 20
        ),
        name="exchange",
    )(integrals, mask, pltpu.with_memory_space_constraint(coeffs, pltpu.MemorySpace.HBM))
    return pl.pallas_call(
        functools.partial(finish_kernel, float(depth) ** -0.5),
        grid=(lcols // WIDE,),
        out_shape=jax.ShapeDtypeStruct((mrows, lcols), jnp.float32),
        in_specs=[
            pl.BlockSpec((mrows, WIDE), lambda n: (0, n)),
            pl.BlockSpec((mrows, 3 * SPAN), lambda n: (0, 0)),
            pl.BlockSpec((2 * SPAN, WIDE), lambda n: (0, n)),
        ],
        out_specs=pl.BlockSpec((mrows, WIDE), lambda n: (0, n)),
        compiler_params=pltpu.CompilerParams(vmem_limit_bytes=14 << 20),
        name="finish",
    )(*partial)


def solution(mesh):
    in_specs = (P(None, None, "rows", "loop"), P(None, "rows", "loop"), P("loop", None))
    out_specs = P("rows", "loop")
    body = functools.partial(local, mesh.shape["loop"], mesh.shape["rows"])
    return jax.shard_map(body, mesh=mesh, in_specs=in_specs, out_specs=out_specs, check_vma=False)
```

```python
import functools

import jax
import jax.numpy as jnp
from jax import lax
from jax.experimental import pallas as pl
from jax.experimental.pallas import tpu as pltpu
from jax.sharding import PartitionSpec as P

TILE = 128
WIDE = 2 * TILE
CHUNK = 64
SPAN = 256
DEEP = 512
HOP = 4
REACH = 3
SLOTS = 8
BUFFERS = 6
BROAD = 512
MESH = pl.DeviceIdType.MESH


def split(x):
    high = x.astype(jnp.bfloat16)
    low = (x - high.astype(jnp.float32)).astype(jnp.bfloat16)
    return high, low


def ring_place(pair, pairs):
    if pairs == 4:
        return pair + (pair // 2) * (1 - 2 * lax.rem(pair, 2))
    return pair


def place_of(part, tile, block, parts, tiles, norbit):
    inner = tile * norbit + block * TILE
    last = block * (tiles * TILE) + tile * TILE
    if isinstance(part, int):
        return part * tiles * norbit + (inner if part < parts - 1 else last)
    return part * (tiles * norbit) + jnp.where(part < parts - 1, inner, last)


def plan(parts, tiles, norbit, lag, last_done):
    groups, blocks = parts * norbit // SPAN, norbit // TILE
    starts, free = [], 0
    for g in range(groups - 1):
        last = max(
            place_of(h // blocks, tiles - 1, h % blocks, parts, tiles, norbit) + TILE - 1 for h in (2 * g, 2 * g + 1)
        )
        starts.append(max(last // CHUNK + lag, free))
        free = starts[-1] + 1 + 2 * tiles
    return starts + [max(last_done, free)]


def exchange_kernel(
    loops, row_count, integrals_ref, mask_ref, coeffs_ref, acc_ref, left_ref, right_ref,
    own, pin, sin, cols, high_ref, low_ref, tile, spare, tile_sem, load_sem,
    up_send, up_recv, dn_send, dn_recv, ch_send, ch_recv, pt_send, pt_recv,
):
    nslab, naux, mrows, lcols = integrals_ref.shape
    norbit = coeffs_ref.shape[1]
    parts = nslab * naux
    tiles = mrows // WIDE
    blocks = norbit // TILE
    tile_count = parts * tiles
    deep = tile.shape[2]
    cuts = lcols // deep
    buffers = tile.shape[0]
    count = own.shape[0] // CHUNK
    ring = pin.shape[0] // CHUNK
    pairs = row_count // 2
    r, l = lax.axis_index("rows"), lax.axis_index("loop")
    pair, core = r // 2, lax.rem(r, 2)
    partner = r + 1 - 2 * core
    turn = 1 - 2 * core
    place = ring_place(pair, pairs)
    far = lax.rem((place - ring_place(l, pairs)) * turn + pairs, pairs)
    ahead = ring_place(lax.rem(place + turn + pairs, pairs), pairs) * 2 + core
    behind = ring_place(lax.rem(place - turn + pairs, pairs), pairs) * 2 + core

    def deep_of(q):
        return pl.ds(pl.multiple_of(q * deep, deep), deep)

    def row_of(part, m, block):
        return pl.ds(pl.multiple_of(place_of(part, m, block, parts, tiles, norbit), TILE), TILE)

    def fetch(u, q):
        part, m = u // tiles, lax.rem(u, tiles)
        slot = lax.rem(u * cuts + q, buffers)
        return pltpu.make_async_copy(
            integrals_ref.at[
                part // naux, lax.rem(part, naux), pl.ds(pl.multiple_of(m * WIDE, WIDE), WIDE), deep_of(q)
            ],
            tile.at[slot],
            tile_sem.at[slot],
        )

    def fetch_next(u, q):
        i = u * cuts + q + buffers

        @pl.when(i < tile_count * cuts)
        def _():
            fetch(i // cuts, lax.rem(i, cuts)).start()

    ranges = ((0, SPAN), (SPAN, norbit))

    def landing(q, k):
        low, high = ranges[k]
        if spare.shape == coeffs_ref.shape:
            return spare.at[deep_of(q), low:high]
        first, rows = q * deep // mrows, lax.rem(q * deep, mrows)
        at = pl.ds(pl.multiple_of(first * norbit + low, TILE), high - low)
        return acc_ref.at[pl.ds(pl.multiple_of(rows, deep), deep), at]

    def load(q, k):
        return pltpu.make_async_copy(
            coeffs_ref.at[deep_of(q), ranges[k][0] : ranges[k][1]], landing(q, k), load_sem.at[k, q]
        )

    def prepare(q, k):
        load(q, k).wait()
        rows = slice(*ranges[k])
        held = landing(q, k)
        for n in range(deep // 256):
            at = pl.ds(pl.multiple_of(q * deep + n * 256, 256), 256)
            high_ref[rows, at], low_ref[rows, at] = split(held[n * 256 : (n + 1) * 256, :].T)

    def half(u, q, first, last):
        part, m = u // tiles, lax.rem(u, tiles)
        slab = part // naux
        own_blocks = range(first // TILE, last // TILE)
        if first == 0:
            fetch(u, q).wait()

        @pl.when(q == 0)
        def _():
            for b in own_blocks:
                own[row_of(part, m, b), :] = jnp.zeros((TILE, WIDE), jnp.float32)

        def piece(i, j):
            keep = mask_ref[slab, m * (WIDE // TILE) + i, q * (deep // TILE) + j].astype(jnp.float32)
            return tile[lax.rem(u * cuts + q, buffers), i * TILE : (i + 1) * TILE, j * TILE : (j + 1) * TILE] * keep

        held = jnp.concatenate(
            [jnp.concatenate([piece(i, j) for j in range(deep // TILE)], axis=1) for i in range(WIDE // TILE)], axis=0
        )
        high, low = split(held)

        def times(a, b):
            return lax.dot_general(a, b, (((1,), (1,)), ((), ())), preferred_element_type=jnp.float32)

        at = deep_of(q)
        upper, lower = high_ref[first:last, at], low_ref[first:last, at]
        value = times(upper, high) + times(upper, low) + times(lower, high)
        for b in own_blocks:
            rows = row_of(part, m, b)
            own[rows, :] = own[rows, :] + value[b * TILE - first : (b + 1) * TILE - first]

        if last == norbit:
            fetch_next(u, q)

    for q in range(cuts):
        load(q, 0).start()
        fetch(0, q).start()
    for q in range(cuts):
        load(q, 1).start()
    for i in range(cuts, buffers):
        fetch(i // cuts, i % cuts).start()

    barrier = pltpu.get_barrier_semaphore()
    for other in (partner, ahead, behind):
        pl.semaphore_signal(barrier, inc=1, device_id={"rows": other}, device_id_type=MESH)

    @pl.when(l > 0)
    def _():
        pl.semaphore_signal(barrier, inc=1, device_id={"loop": l - 1}, device_id_type=MESH)

    @pl.when(l < loops - 1)
    def _():
        pl.semaphore_signal(barrier, inc=1, device_id={"loop": l + 1}, device_id_type=MESH)

    @pl.loop(0, cuts)
    def _(q):
        prepare(q, 0)
        half(0, q, 0, SPAN)

    neighbours = jnp.where(l > 0, 1, 0) + jnp.where(l < loops - 1, 1, 0)
    pl.semaphore_wait(barrier, 3 + neighbours)

    def rows_of(j):
        return pl.ds(pl.multiple_of(j * CHUNK, CHUNK), CHUNK)

    def slot_of(j):
        return pl.ds(pl.multiple_of(lax.rem(j, ring) * CHUNK, CHUNK), CHUNK)

    def copy(src, dst, send, recv, j, target):
        return pltpu.make_async_remote_copy(
            src_ref=src, dst_ref=dst, send_sem=send.at[lax.rem(j, SLOTS)], recv_sem=recv.at[j],
            device_id=target, device_id_type=MESH,
        )

    def up(j):
        return copy(pin.at[slot_of(j)], pin.at[slot_of(j)], up_send, up_recv, j, {"loop": l + 1})

    def down(j):
        return copy(sin.at[slot_of(j)], sin.at[slot_of(j)], dn_send, dn_recv, j, {"loop": l - 1})

    def chain(j):
        ref = cols.at[core, rows_of(j)]
        return copy(ref, ref, ch_send, ch_recv, j, {"rows": ahead})

    def share(j):
        ref = cols.at[core, rows_of(j)]
        return copy(ref, ref, pt_send, pt_recv, j, {"rows": partner})

    def taken(j):
        ref = cols.at[1 - core, rows_of(j)]
        return copy(ref, ref, pt_send, pt_recv, j, {"rows": partner})

    def send(make, j):
        @pl.when(j >= SLOTS)
        def _():
            make(j - SLOTS).wait_send()

        make(j).start()

    def line(held, make, j, first, last):
        @pl.when((j >= 0) & (j < count))
        def _():
            at, slot = rows_of(j), slot_of(j)

            @pl.when(first)
            def _():
                held[slot, :] = own[at, :]

            @pl.when(jnp.logical_not(first))
            def _():
                make(j).wait_recv()
                held[slot, :] = held[slot, :] + own[at, :]

            @pl.when(jnp.logical_not(last))
            def _():
                send(make, j)

    settle = HOP * jnp.maximum(l, loops - 1 - l)
    lag = HOP * (loops - 1) + REACH * pairs
    starts = plan(parts, tiles, norbit, lag, count - 1 + HOP * (loops - 1))
    groups = len(starts)
    total_steps = max(count + lag, starts[-1] + 1)
    final = count - 2 * TILE * tiles // CHUNK

    def multiply(g, n):
        @pl.when(n == 0)
        def _():
            @pl.loop(0, tiles)
            def _(m):
                mine = pl.ds(pl.multiple_of(m * WIDE, WIDE), WIDE)
                for h in range(2):
                    block = 2 * g + h
                    high, low = split(own[row_of(block // blocks, m, lax.rem(block, blocks)), :].T)
                    left_ref[mine, h * TILE : (h + 1) * TILE] = high
                    left_ref[mine, SPAN + h * TILE : SPAN + (h + 1) * TILE] = high
                    left_ref[mine, 2 * SPAN + h * TILE : 2 * SPAN + (h + 1) * TILE] = low

        @pl.when(n > 0)
        def _():
            held, m = (n - 1) // tiles, lax.rem(n - 1, tiles)
            both = []
            for h in range(2):
                block = 2 * g + h
                both.append(cols[held, row_of(block // blocks, m, lax.rem(block, blocks)), :])
            high, low = split(jnp.concatenate(both, axis=0))
            right = jnp.concatenate([high, low, high], axis=0)
            theirs = pl.ds(pl.multiple_of((n - 1) * WIDE, WIDE), WIDE)

            @pl.when(g == 0)
            def _():
                acc_ref[:, theirs] = jnp.zeros((mrows, WIDE), jnp.float32)

            acc_ref[:, theirs] = acc_ref[:, theirs] + jnp.dot(left_ref[...], right, preferred_element_type=jnp.float32)

    def step(t, carry):
        line(pin, up, t - HOP * l, l == 0, l == loops - 1)
        line(sin, down, t - HOP * (loops - 1 - l), l == loops - 1, l == 0)

        done = t - settle

        @pl.when((done >= 0) & (done < count))
        def _():
            at, slot = rows_of(done), slot_of(done)
            total = pin[slot, :] + (sin[slot, :] - own[at, :])
            own[at, :] = total

            @pl.when(far == 0)
            def _():
                cols[core, at, :] = total

        passed = done - REACH * far

        @pl.when((passed >= 0) & (passed < count))
        def _():
            @pl.when(far > 0)
            def _():
                chain(passed).wait_recv()

            @pl.when(far < pairs - 1)
            def _():
                send(chain, passed)

            send(share, passed)

        ready = done - REACH * pairs

        @pl.when((ready >= 0) & (ready < count))
        def _():
            taken(ready).wait_recv()

        @pl.when((ready >= final) & (ready < count))
        def _():
            off = (ready - final) * CHUNK
            k = off // (tiles * TILE) * TILE + lax.rem(off, TILE)
            m = lax.rem(off // TILE, tiles)
            for held in range(2):
                high, low = split(cols[held, rows_of(ready), :])
                theirs = pl.ds(pl.multiple_of(held * mrows + m * WIDE, WIDE), WIDE)
                right_ref[pl.ds(pl.multiple_of(k, CHUNK), CHUNK), theirs] = high
                right_ref[pl.ds(pl.multiple_of(SPAN + k, CHUNK), CHUNK), theirs] = low

        g, begin = -1, 0
        for k, at in enumerate(starts):
            g = g + jnp.where(t >= at, 1, 0)
            begin = begin + jnp.where(t >= at, at - (starts[k - 1] if k else 0), 0)

        @pl.when((g >= 0) & (t - begin <= jnp.where(g < groups - 1, 2 * tiles, 0)))
        def _():
            multiply(g, t - begin)

        @pl.when(t < cuts)
        def _():
            prepare(t, 1)
            half(0, t, SPAN, norbit)

        later, q = 1 + (t - cuts) // (cuts + 1), lax.rem(t - cuts, cuts + 1)

        @pl.when((t >= cuts) & (later < tile_count) & (q < cuts))
        def _():
            half(later, q, 0, norbit)

        return carry

    lax.fori_loop(0, total_steps, step, 0)

    def drain(i, carry):
        j = count - SLOTS + i

        @pl.when(l < loops - 1)
        def _():
            up(j).wait_send()

        @pl.when(l > 0)
        def _():
            down(j).wait_send()

        @pl.when(far < pairs - 1)
        def _():
            chain(j).wait_send()

        share(j).wait_send()
        return carry

    lax.fori_loop(0, SLOTS, drain, 0)


def finish_kernel(scale, acc_ref, left_ref, right_ref, out_ref):
    broad = out_ref.shape[1]
    at = pl.ds(pl.multiple_of(pl.program_id(0) * broad, broad), broad)
    right = jnp.concatenate([right_ref[:, at], right_ref[:SPAN, at]], axis=0)
    value = acc_ref[:, at] + jnp.dot(left_ref[...], right, preferred_element_type=jnp.float32)
    out_ref[...] = value * scale


def local(loops, row_count, integrals, mask, coeffs):
    nslab, naux, mrows, lcols = integrals.shape
    norbit = coeffs.shape[1]
    depth = nslab * naux * norbit
    tiles = mrows // WIDE
    count = depth * tiles * WIDE // (CHUNK * WIDE)
    assert lcols == 2 * mrows and row_count == 2 * loops and mrows % WIDE == 0
    assert norbit % TILE == 0 and norbit >= SPAN and depth % SPAN == 0
    deep = min(DEEP, lcols)
    cuts = lcols // deep
    buffers = min(BUFFERS, nslab * naux * tiles * cuts)
    assert cuts + 1 <= norbit // CHUNK and cuts <= min(buffers, SPAN // CHUNK) and norbit > SPAN
    spare = (8, 128) if 2 * norbit <= lcols and mrows % deep == 0 else (lcols, norbit)
    broad = min(BROAD, lcols)
    ring = min(count, max(SLOTS + 2 * HOP, HOP * (loops - 1)) + 2)
    dma = pltpu.SemaphoreType.DMA
    vmem = pl.BlockSpec(memory_space=pltpu.VMEM)
    held = functools.partial(pltpu.with_memory_space_constraint, memory_space=pltpu.MemorySpace.HBM)
    partial = pl.pallas_call(
        functools.partial(exchange_kernel, loops, row_count),
        out_shape=[
            jax.ShapeDtypeStruct((mrows, lcols), jnp.float32),
            jax.ShapeDtypeStruct((mrows, 3 * SPAN), jnp.bfloat16),
            jax.ShapeDtypeStruct((2 * SPAN, lcols), jnp.bfloat16),
        ],
        in_specs=[
            pl.BlockSpec(memory_space=pl.ANY),
            pl.BlockSpec(memory_space=pltpu.SMEM),
            pl.BlockSpec(memory_space=pl.ANY),
        ],
        out_specs=[vmem] * 3,
        scratch_shapes=[
            pltpu.VMEM((depth * tiles, WIDE), jnp.float32),
            pltpu.VMEM((ring * CHUNK, WIDE), jnp.float32),
            pltpu.VMEM((ring * CHUNK, WIDE), jnp.float32),
            pltpu.VMEM((2, depth * tiles, WIDE), jnp.float32),
            pltpu.VMEM((norbit, lcols), jnp.bfloat16),
            pltpu.VMEM((norbit, lcols), jnp.bfloat16),
            pltpu.VMEM((buffers, WIDE, deep), jnp.float32),
            pltpu.VMEM(spare, jnp.float32),
            dma((buffers,)),
            dma((2, cuts)),
        ]
        + [dma((SLOTS,)), dma((count,))] * 4,
        compiler_params=pltpu.CompilerParams(
            collective_id=0, has_side_effects=True, vmem_limit_bytes=42 << 20
        ),
        name="exchange",
    )(integrals, held(mask), held(coeffs))
    return pl.pallas_call(
        functools.partial(finish_kernel, float(depth) ** -0.5),
        grid=(lcols // broad,),
        out_shape=jax.ShapeDtypeStruct((mrows, lcols), jnp.float32),
        in_specs=[vmem] * 3,
        out_specs=pl.BlockSpec((mrows, broad), lambda n: (0, n)),
        compiler_params=pltpu.CompilerParams(vmem_limit_bytes=14 << 20),
        name="finish",
    )(*partial)


def solution(mesh):
    in_specs = (P(None, None, "rows", "loop"), P(None, "rows", "loop"), P("loop", None))
    out_specs = P("rows", "loop")
    body = functools.partial(local, mesh.shape["loop"], mesh.shape["rows"])
    return jax.shard_map(body, mesh=mesh, in_specs=in_specs, out_specs=out_specs, check_vma=False)
```

```python
import functools

import jax
import jax.numpy as jnp
from jax import lax
from jax.experimental import pallas as pl
from jax.experimental.pallas import tpu as pltpu
from jax.sharding import PartitionSpec as P

TILE = 128
WIDE = 2 * TILE
CHUNK = 64
SPAN = 256
DEEP = 512
HOP = 3
REACH = 3
SLOTS = 8
BUFFERS = 6
BROAD = 512
MESH = pl.DeviceIdType.MESH


def split(x):
    high = x.astype(jnp.bfloat16)
    low = (x - high.astype(jnp.float32)).astype(jnp.bfloat16)
    return high, low


def ring_place(pair, pairs):
    if pairs == 4:
        return pair + (pair // 2) * (1 - 2 * lax.rem(pair, 2))
    return pair


def place_of(part, tile, block, parts, tiles, norbit):
    inner = tile * norbit + block * TILE
    last = block * (tiles * TILE) + tile * TILE
    if isinstance(part, int):
        return part * tiles * norbit + (inner if part < parts - 1 else last)
    return part * (tiles * norbit) + jnp.where(part < parts - 1, inner, last)


def plan(parts, tiles, norbit, lag, last_done):
    groups, blocks = parts * norbit // SPAN, norbit // TILE
    starts, free = [], 0
    for g in range(groups - 1):
        last = max(
            place_of(h // blocks, tiles - 1, h % blocks, parts, tiles, norbit) + TILE - 1 for h in (2 * g, 2 * g + 1)
        )
        starts.append(max(last // CHUNK + lag, free))
        free = starts[-1] + 1 + 2 * tiles
    return starts + [max(last_done, free)]


def exchange_kernel(
    loops, row_count, integrals_ref, mask_ref, coeffs_ref, acc_ref, left_ref, right_ref,
    own, pin, sin, cols, high_ref, low_ref, tile, spare, tile_sem, load_sem,
    keep_ref, keep_sem, up_send, up_recv, dn_send, dn_recv, ch_send, ch_recv, pt_send, pt_recv, bk_send,
):
    nslab, naux, mrows, lcols = integrals_ref.shape
    norbit = coeffs_ref.shape[1]
    parts = nslab * naux
    tiles = mrows // WIDE
    blocks = norbit // TILE
    tile_count = parts * tiles
    deep = tile.shape[2]
    cuts = lcols // deep
    buffers = tile.shape[0]
    count = own.shape[0] // CHUNK
    ring = pin.shape[0] // CHUNK
    pairs = row_count // 2
    r, l = lax.axis_index("rows"), lax.axis_index("loop")
    pair, core = r // 2, lax.rem(r, 2)
    partner = r + 1 - 2 * core
    turn = 1 - 2 * core
    place = ring_place(pair, pairs)
    far = lax.rem((place - ring_place(l, pairs)) * turn + pairs, pairs)
    ahead = ring_place(lax.rem(place + turn + pairs, pairs), pairs) * 2 + core
    behind = ring_place(lax.rem(place - turn + pairs, pairs), pairs) * 2 + core
    longest = pairs // 2
    hops = jnp.where(far <= longest, far, pairs - far)
    forward = far < longest
    backward = ((far == 0) & (longest < pairs - 1)) | (far > longest + 1)

    def deep_of(q):
        return pl.ds(pl.multiple_of(q * deep, deep), deep)

    def row_of(part, m, block):
        return pl.ds(pl.multiple_of(place_of(part, m, block, parts, tiles, norbit), TILE), TILE)

    def fetch(u, q):
        part, m = u // tiles, lax.rem(u, tiles)
        slot = lax.rem(u * cuts + q, buffers)
        return pltpu.make_async_copy(
            integrals_ref.at[
                part // naux, lax.rem(part, naux), pl.ds(pl.multiple_of(m * WIDE, WIDE), WIDE), deep_of(q)
            ],
            tile.at[slot],
            tile_sem.at[slot],
        )

    def fetch_next(u, q):
        i = u * cuts + q + buffers

        @pl.when(i < tile_count * cuts)
        def _():
            fetch(i // cuts, lax.rem(i, cuts)).start()

    ranges = ((0, SPAN), (SPAN, norbit))

    def landing(q, k):
        low, high = ranges[k]
        if spare.shape == coeffs_ref.shape:
            return spare.at[deep_of(q), low:high]
        first, rows = q * deep // mrows, lax.rem(q * deep, mrows)
        at = pl.ds(pl.multiple_of(first * norbit + low, TILE), high - low)
        return acc_ref.at[pl.ds(pl.multiple_of(rows, deep), deep), at]

    def load(q, k):
        return pltpu.make_async_copy(
            coeffs_ref.at[deep_of(q), ranges[k][0] : ranges[k][1]], landing(q, k), load_sem.at[k, q]
        )

    def prepare(q, k):
        load(q, k).wait()
        rows = slice(*ranges[k])
        held = landing(q, k)
        for n in range(deep // 256):
            at = pl.ds(pl.multiple_of(q * deep + n * 256, 256), 256)
            high_ref[rows, at], low_ref[rows, at] = split(held[n * 256 : (n + 1) * 256, :].T)

    def half(u, q, first, last):
        part, m = u // tiles, lax.rem(u, tiles)
        slab = part // naux
        own_blocks = range(first // TILE, last // TILE)
        if first == 0:
            fetch(u, q).wait()

        @pl.when(q == 0)
        def _():
            for b in own_blocks:
                own[row_of(part, m, b), :] = jnp.zeros((TILE, WIDE), jnp.float32)

        def piece(i, j):
            keep = keep_ref[slab, m * (WIDE // TILE) + i, q * (deep // TILE) + j].astype(jnp.float32)
            return tile[lax.rem(u * cuts + q, buffers), i * TILE : (i + 1) * TILE, j * TILE : (j + 1) * TILE] * keep

        held = jnp.concatenate(
            [jnp.concatenate([piece(i, j) for j in range(deep // TILE)], axis=1) for i in range(WIDE // TILE)], axis=0
        )
        high, low = split(held)

        def times(a, b):
            return lax.dot_general(a, b, (((1,), (1,)), ((), ())), preferred_element_type=jnp.float32)

        at = deep_of(q)
        upper, lower = high_ref[first:last, at], low_ref[first:last, at]
        value = times(upper, high) + times(upper, low) + times(lower, high)
        for b in own_blocks:
            rows = row_of(part, m, b)
            own[rows, :] = own[rows, :] + value[b * TILE - first : (b + 1) * TILE - first]

        if last == norbit:
            fetch_next(u, q)

    taken_mask = pltpu.make_async_copy(mask_ref, keep_ref, keep_sem)
    taken_mask.start()
    for q in range(cuts):
        load(q, 0).start()
        fetch(0, q).start()
    for q in range(cuts):
        load(q, 1).start()
    for i in range(cuts, buffers):
        fetch(i // cuts, i % cuts).start()

    barrier = pltpu.get_barrier_semaphore()
    for other in (partner, ahead, behind):
        pl.semaphore_signal(barrier, inc=1, device_id={"rows": other}, device_id_type=MESH)

    @pl.when(l > 0)
    def _():
        pl.semaphore_signal(barrier, inc=1, device_id={"loop": l - 1}, device_id_type=MESH)

    @pl.when(l < loops - 1)
    def _():
        pl.semaphore_signal(barrier, inc=1, device_id={"loop": l + 1}, device_id_type=MESH)

    taken_mask.wait()

    @pl.loop(0, cuts)
    def _(q):
        prepare(q, 0)
        half(0, q, 0, SPAN)

    neighbours = jnp.where(l > 0, 1, 0) + jnp.where(l < loops - 1, 1, 0)
    pl.semaphore_wait(barrier, 3 + neighbours)

    def rows_of(j):
        return pl.ds(pl.multiple_of(j * CHUNK, CHUNK), CHUNK)

    def slot_of(j):
        return pl.ds(pl.multiple_of(lax.rem(j, ring) * CHUNK, CHUNK), CHUNK)

    def copy(src, dst, send, recv, j, target):
        return pltpu.make_async_remote_copy(
            src_ref=src, dst_ref=dst, send_sem=send.at[lax.rem(j, SLOTS)], recv_sem=recv.at[j],
            device_id=target, device_id_type=MESH,
        )

    def up(j):
        return copy(pin.at[slot_of(j)], pin.at[slot_of(j)], up_send, up_recv, j, {"loop": l + 1})

    def down(j):
        return copy(sin.at[slot_of(j)], sin.at[slot_of(j)], dn_send, dn_recv, j, {"loop": l - 1})

    def chain(j):
        ref = cols.at[core, rows_of(j)]
        return copy(ref, ref, ch_send, ch_recv, j, {"rows": ahead})

    def back(j):
        ref = cols.at[core, rows_of(j)]
        return copy(ref, ref, bk_send, ch_recv, j, {"rows": behind})

    def share(j):
        ref = cols.at[core, rows_of(j)]
        return copy(ref, ref, pt_send, pt_recv, j, {"rows": partner})

    def taken(j):
        ref = cols.at[1 - core, rows_of(j)]
        return copy(ref, ref, pt_send, pt_recv, j, {"rows": partner})

    def send(make, j):
        @pl.when(j >= SLOTS)
        def _():
            make(j - SLOTS).wait_send()

        make(j).start()

    def line(held, make, j, first, last):
        @pl.when((j >= 0) & (j < count))
        def _():
            at, slot = rows_of(j), slot_of(j)

            @pl.when(first)
            def _():
                held[slot, :] = own[at, :]

            @pl.when(jnp.logical_not(first))
            def _():
                make(j).wait_recv()
                held[slot, :] = held[slot, :] + own[at, :]

            @pl.when(jnp.logical_not(last))
            def _():
                send(make, j)

    settle = HOP * jnp.maximum(l, loops - 1 - l)
    lag = HOP * (loops - 1) + REACH * (longest + 1)
    starts = plan(parts, tiles, norbit, lag, count - 1 + HOP * (loops - 1))
    groups = len(starts)
    total_steps = max(count + lag, starts[-1] + 1)
    final = count - 2 * TILE * tiles // CHUNK

    def multiply(g, n):
        @pl.when(n == 0)
        def _():
            @pl.loop(0, tiles)
            def _(m):
                mine = pl.ds(pl.multiple_of(m * WIDE, WIDE), WIDE)
                for h in range(2):
                    block = 2 * g + h
                    high, low = split(own[row_of(block // blocks, m, lax.rem(block, blocks)), :].T)
                    left_ref[mine, h * TILE : (h + 1) * TILE] = high
                    left_ref[mine, SPAN + h * TILE : SPAN + (h + 1) * TILE] = high
                    left_ref[mine, 2 * SPAN + h * TILE : 2 * SPAN + (h + 1) * TILE] = low

        @pl.when(n > 0)
        def _():
            held, m = (n - 1) // tiles, lax.rem(n - 1, tiles)
            both = []
            for h in range(2):
                block = 2 * g + h
                both.append(cols[held, row_of(block // blocks, m, lax.rem(block, blocks)), :])
            high, low = split(jnp.concatenate(both, axis=0))
            right = jnp.concatenate([high, low, high], axis=0)
            theirs = pl.ds(pl.multiple_of((n - 1) * WIDE, WIDE), WIDE)

            @pl.when(g == 0)
            def _():
                acc_ref[:, theirs] = jnp.zeros((mrows, WIDE), jnp.float32)

            acc_ref[:, theirs] = acc_ref[:, theirs] + jnp.dot(left_ref[...], right, preferred_element_type=jnp.float32)

    def step(t, carry):
        line(pin, up, t - HOP * l, l == 0, l == loops - 1)
        line(sin, down, t - HOP * (loops - 1 - l), l == loops - 1, l == 0)

        done = t - settle

        @pl.when((done >= 0) & (done < count))
        def _():
            at, slot = rows_of(done), slot_of(done)
            total = pin[slot, :] + (sin[slot, :] - own[at, :])
            own[at, :] = total

            @pl.when(far == 0)
            def _():
                cols[core, at, :] = total

        passed = done - REACH * hops

        @pl.when((passed >= 0) & (passed < count))
        def _():
            @pl.when(far > 0)
            def _():
                chain(passed).wait_recv()

            @pl.when(forward)
            def _():
                send(chain, passed)

            @pl.when(backward)
            def _():
                send(back, passed)

            send(share, passed)

        ready = done - REACH * (longest + 1)

        @pl.when((ready >= 0) & (ready < count))
        def _():
            taken(ready).wait_recv()

        @pl.when((ready >= final) & (ready < count))
        def _():
            off = (ready - final) * CHUNK
            k = off // (tiles * TILE) * TILE + lax.rem(off, TILE)
            m = lax.rem(off // TILE, tiles)
            for held in range(2):
                high, low = split(cols[held, rows_of(ready), :])
                theirs = pl.ds(pl.multiple_of(held * mrows + m * WIDE, WIDE), WIDE)
                right_ref[pl.ds(pl.multiple_of(k, CHUNK), CHUNK), theirs] = high
                right_ref[pl.ds(pl.multiple_of(SPAN + k, CHUNK), CHUNK), theirs] = low

        g, begin = -1, 0
        for k, at in enumerate(starts):
            g = g + jnp.where(t >= at, 1, 0)
            begin = begin + jnp.where(t >= at, at - (starts[k - 1] if k else 0), 0)

        @pl.when((g >= 0) & (t - begin <= jnp.where(g < groups - 1, 2 * tiles, 0)))
        def _():
            multiply(g, t - begin)

        @pl.when(t < cuts)
        def _():
            prepare(t, 1)
            half(0, t, SPAN, norbit)

        later, q = 1 + (t - cuts) // (cuts + 1), lax.rem(t - cuts, cuts + 1)

        @pl.when((t >= cuts) & (later < tile_count) & (q < cuts))
        def _():
            half(later, q, 0, norbit)

        return carry

    lax.fori_loop(0, total_steps, step, 0)

    def drain(i, carry):
        j = count - SLOTS + i

        @pl.when(l < loops - 1)
        def _():
            up(j).wait_send()

        @pl.when(l > 0)
        def _():
            down(j).wait_send()

        @pl.when(forward)
        def _():
            chain(j).wait_send()

        @pl.when(backward)
        def _():
            back(j).wait_send()

        share(j).wait_send()
        return carry

    lax.fori_loop(0, SLOTS, drain, 0)


def finish_kernel(scale, acc_ref, left_ref, right_ref, out_ref):
    broad = out_ref.shape[1]
    at = pl.ds(pl.multiple_of(pl.program_id(0) * broad, broad), broad)
    right = jnp.concatenate([right_ref[:, at], right_ref[:SPAN, at]], axis=0)
    value = acc_ref[:, at] + jnp.dot(left_ref[...], right, preferred_element_type=jnp.float32)
    out_ref[...] = value * scale


def local(loops, row_count, integrals, mask, coeffs):
    nslab, naux, mrows, lcols = integrals.shape
    norbit = coeffs.shape[1]
    depth = nslab * naux * norbit
    tiles = mrows // WIDE
    count = depth * tiles * WIDE // (CHUNK * WIDE)
    assert lcols == 2 * mrows and row_count == 2 * loops and mrows % WIDE == 0
    assert norbit % TILE == 0 and norbit >= SPAN and depth % SPAN == 0
    deep = min(DEEP, lcols)
    cuts = lcols // deep
    buffers = min(BUFFERS, nslab * naux * tiles * cuts)
    assert cuts + 1 <= norbit // CHUNK and cuts <= min(buffers, SPAN // CHUNK) and norbit > SPAN
    spare = (8, 128) if 2 * norbit <= lcols and mrows % deep == 0 else (lcols, norbit)
    broad = min(BROAD, lcols)
    ring = min(count, max(SLOTS + 2 * HOP, HOP * (loops - 1)) + 2)
    dma = pltpu.SemaphoreType.DMA
    vmem = pl.BlockSpec(memory_space=pltpu.VMEM)
    held = functools.partial(pltpu.with_memory_space_constraint, memory_space=pltpu.MemorySpace.HBM)
    partial = pl.pallas_call(
        functools.partial(exchange_kernel, loops, row_count),
        out_shape=[
            jax.ShapeDtypeStruct((mrows, lcols), jnp.float32),
            jax.ShapeDtypeStruct((mrows, 3 * SPAN), jnp.bfloat16),
            jax.ShapeDtypeStruct((2 * SPAN, lcols), jnp.bfloat16),
        ],
        in_specs=[
            pl.BlockSpec(memory_space=pl.ANY),
            pl.BlockSpec(memory_space=pl.ANY),
            pl.BlockSpec(memory_space=pl.ANY),
        ],
        out_specs=[vmem] * 3,
        scratch_shapes=[
            pltpu.VMEM((depth * tiles, WIDE), jnp.float32),
            pltpu.VMEM((ring * CHUNK, WIDE), jnp.float32),
            pltpu.VMEM((ring * CHUNK, WIDE), jnp.float32),
            pltpu.VMEM((2, depth * tiles, WIDE), jnp.float32),
            pltpu.VMEM((norbit, lcols), jnp.bfloat16),
            pltpu.VMEM((norbit, lcols), jnp.bfloat16),
            pltpu.VMEM((buffers, WIDE, deep), jnp.float32),
            pltpu.VMEM(spare, jnp.float32),
            dma((buffers,)),
            dma((2, cuts)),
        ]
        + [pltpu.SMEM(mask.shape, mask.dtype), dma]
        + [dma((SLOTS,)), dma((count,))] * 4
        + [dma((SLOTS,))],
        compiler_params=pltpu.CompilerParams(
            collective_id=0, has_side_effects=True, vmem_limit_bytes=42 << 20
        ),
        name="exchange",
    )(integrals, held(mask), held(coeffs))
    return pl.pallas_call(
        functools.partial(finish_kernel, float(depth) ** -0.5),
        grid=(lcols // broad,),
        out_shape=jax.ShapeDtypeStruct((mrows, lcols), jnp.float32),
        in_specs=[vmem] * 3,
        out_specs=pl.BlockSpec((mrows, broad), lambda n: (0, n)),
        compiler_params=pltpu.CompilerParams(vmem_limit_bytes=14 << 20),
        name="finish",
    )(*partial)


def solution(mesh):
    in_specs = (P(None, None, "rows", "loop"), P(None, "rows", "loop"), P("loop", None))
    out_specs = P("rows", "loop")
    body = functools.partial(local, mesh.shape["loop"], mesh.shape["rows"])
    return jax.shard_map(body, mesh=mesh, in_specs=in_specs, out_specs=out_specs, check_vma=False)
```

```python
import functools

import jax
import jax.numpy as jnp
from jax import lax
from jax.experimental import pallas as pl
from jax.experimental.pallas import tpu as pltpu
from jax.sharding import PartitionSpec as P

TILE = 128
WIDE = 2 * TILE
CHUNK = 64
SPAN = 256
DEEP = 512
HOP = 3
REACH = 3
SLOTS = 8
BUFFERS = 6
BROAD = 512
MESH = pl.DeviceIdType.MESH


def split(x):
    high = x.astype(jnp.bfloat16)
    low = (x - high.astype(jnp.float32)).astype(jnp.bfloat16)
    return high, low


def ring_place(pair, pairs):
    if pairs == 4:
        return pair + (pair // 2) * (1 - 2 * lax.rem(pair, 2))
    return pair


def place_of(part, tile, block, parts, tiles, norbit):
    inner = tile * norbit + block * TILE
    last = block * (tiles * TILE) + tile * TILE
    if isinstance(part, int):
        return part * tiles * norbit + (inner if part < parts - 1 else last)
    return part * (tiles * norbit) + jnp.where(part < parts - 1, inner, last)


def plan(parts, tiles, norbit, lag, last_done, free):
    groups, blocks = parts * norbit // SPAN, norbit // TILE
    starts = []
    for g in range(groups - 1):
        last = max(
            place_of(h // blocks, tiles - 1, h % blocks, parts, tiles, norbit) + TILE - 1 for h in (2 * g, 2 * g + 1)
        )
        starts.append(max(last // CHUNK + lag, free))
        free = starts[-1] + 1 + 2 * tiles
    return starts + [max(last_done, free)]


def exchange_kernel(
    loops, row_count, integrals_ref, mask_ref, coeffs_ref, acc_ref, left_ref, right_ref,
    own, pin, sin, cols, high_ref, low_ref, tile, spare, tile_sem, load_sem,
    keep_ref, keep_sem, up_send, up_recv, dn_send, dn_recv, ch_send, ch_recv, pt_send, pt_recv, bk_send,
):
    nslab, naux, mrows, lcols = integrals_ref.shape
    norbit = coeffs_ref.shape[1]
    parts = nslab * naux
    tiles = mrows // WIDE
    blocks = norbit // TILE
    tile_count = parts * tiles
    deep = tile.shape[2]
    cuts = lcols // deep
    buffers = tile.shape[0]
    count = own.shape[0] // CHUNK
    ring = pin.shape[0] // CHUNK
    pairs = row_count // 2
    r, l = lax.axis_index("rows"), lax.axis_index("loop")
    pair, core = r // 2, lax.rem(r, 2)
    partner = r + 1 - 2 * core
    turn = 1 - 2 * core
    place = ring_place(pair, pairs)
    far = lax.rem((place - ring_place(l, pairs)) * turn + pairs, pairs)
    ahead = ring_place(lax.rem(place + turn + pairs, pairs), pairs) * 2 + core
    behind = ring_place(lax.rem(place - turn + pairs, pairs), pairs) * 2 + core
    longest = pairs // 2
    hops = jnp.where(far <= longest, far, pairs - far)
    forward = far < longest
    backward = ((far == 0) & (longest < pairs - 1)) | (far > longest + 1)

    def deep_of(q):
        return pl.ds(pl.multiple_of(q * deep, deep), deep)

    def row_of(part, m, block):
        return pl.ds(pl.multiple_of(place_of(part, m, block, parts, tiles, norbit), TILE), TILE)

    def fetch(u, q):
        part, m = u // tiles, lax.rem(u, tiles)
        slot = lax.rem(u * cuts + q, buffers)
        return pltpu.make_async_copy(
            integrals_ref.at[
                part // naux, lax.rem(part, naux), pl.ds(pl.multiple_of(m * WIDE, WIDE), WIDE), deep_of(q)
            ],
            tile.at[slot],
            tile_sem.at[slot],
        )

    def fetch_next(u, q):
        i = u * cuts + q + buffers

        @pl.when(i < tile_count * cuts)
        def _():
            fetch(i // cuts, lax.rem(i, cuts)).start()

    ranges = ((0, SPAN), (SPAN, norbit))

    def landing(q, k):
        low, high = ranges[k]
        if spare.shape == coeffs_ref.shape:
            return spare.at[deep_of(q), low:high]
        first, rows = q * deep // mrows, lax.rem(q * deep, mrows)
        at = pl.ds(pl.multiple_of(first * norbit + low, TILE), high - low)
        return acc_ref.at[pl.ds(pl.multiple_of(rows, deep), deep), at]

    def load(q, k):
        return pltpu.make_async_copy(
            coeffs_ref.at[deep_of(q), ranges[k][0] : ranges[k][1]], landing(q, k), load_sem.at[k, q]
        )

    def prepare(q, k):
        load(q, k).wait()
        rows = slice(*ranges[k])
        held = landing(q, k)
        for n in range(deep // 256):
            at = pl.ds(pl.multiple_of(q * deep + n * 256, 256), 256)
            high_ref[rows, at], low_ref[rows, at] = split(held[n * 256 : (n + 1) * 256, :].T)

    def half(u, q, first, last):
        part, m = u // tiles, lax.rem(u, tiles)
        slab = part // naux
        own_blocks = range(first // TILE, last // TILE)
        if first == 0:
            fetch(u, q).wait()

        @pl.when(q == 0)
        def _():
            for b in own_blocks:
                own[row_of(part, m, b), :] = jnp.zeros((TILE, WIDE), jnp.float32)

        def piece(i, j):
            keep = keep_ref[slab, m * (WIDE // TILE) + i, q * (deep // TILE) + j].astype(jnp.float32)
            return tile[lax.rem(u * cuts + q, buffers), i * TILE : (i + 1) * TILE, j * TILE : (j + 1) * TILE] * keep

        held = jnp.concatenate(
            [jnp.concatenate([piece(i, j) for j in range(deep // TILE)], axis=1) for i in range(WIDE // TILE)], axis=0
        )
        high, low = split(held)

        def times(a, b):
            return lax.dot_general(a, b, (((1,), (1,)), ((), ())), preferred_element_type=jnp.float32)

        at = deep_of(q)
        upper, lower = high_ref[first:last, at], low_ref[first:last, at]
        value = times(upper, high) + times(upper, low) + times(lower, high)
        for b in own_blocks:
            rows = row_of(part, m, b)
            own[rows, :] = own[rows, :] + value[b * TILE - first : (b + 1) * TILE - first]

        if last == norbit:
            fetch_next(u, q)

    taken_mask = pltpu.make_async_copy(mask_ref, keep_ref, keep_sem)
    taken_mask.start()
    for q in range(cuts):
        load(q, 0).start()
        fetch(0, q).start()
    for q in range(cuts):
        load(q, 1).start()
    for i in range(cuts, buffers):
        fetch(i // cuts, i % cuts).start()

    barrier = pltpu.get_barrier_semaphore()
    for other in (partner, ahead, behind):
        pl.semaphore_signal(barrier, inc=1, device_id={"rows": other}, device_id_type=MESH)

    @pl.when(l > 0)
    def _():
        pl.semaphore_signal(barrier, inc=1, device_id={"loop": l - 1}, device_id_type=MESH)

    @pl.when(l < loops - 1)
    def _():
        pl.semaphore_signal(barrier, inc=1, device_id={"loop": l + 1}, device_id_type=MESH)

    taken_mask.wait()

    @pl.loop(0, cuts)
    def _(q):
        prepare(q, 0)
        half(0, q, 0, SPAN)

    neighbours = jnp.where(l > 0, 1, 0) + jnp.where(l < loops - 1, 1, 0)
    pl.semaphore_wait(barrier, 3 + neighbours)

    def rows_of(j):
        return pl.ds(pl.multiple_of(j * CHUNK, CHUNK), CHUNK)

    def slot_of(j):
        return pl.ds(pl.multiple_of(lax.rem(j, ring) * CHUNK, CHUNK), CHUNK)

    def copy(src, dst, send, recv, j, target):
        return pltpu.make_async_remote_copy(
            src_ref=src, dst_ref=dst, send_sem=send.at[lax.rem(j, SLOTS)], recv_sem=recv.at[lax.rem(j, recv.shape[0])],
            device_id=target, device_id_type=MESH,
        )

    def up(j):
        return copy(pin.at[slot_of(j)], pin.at[slot_of(j)], up_send, up_recv, j, {"loop": l + 1})

    def down(j):
        return copy(sin.at[slot_of(j)], sin.at[slot_of(j)], dn_send, dn_recv, j, {"loop": l - 1})

    def chain(j):
        ref = cols.at[core, rows_of(j)]
        return copy(ref, ref, ch_send, ch_recv, j, {"rows": ahead})

    def back(j):
        ref = cols.at[core, rows_of(j)]
        return copy(ref, ref, bk_send, ch_recv, j, {"rows": behind})

    def share(j):
        ref = cols.at[core, rows_of(j)]
        return copy(ref, ref, pt_send, pt_recv, j, {"rows": partner})

    def taken(j):
        ref = cols.at[1 - core, rows_of(j)]
        return copy(ref, ref, pt_send, pt_recv, j, {"rows": partner})

    def send(make, j):
        @pl.when(j >= SLOTS)
        def _():
            make(j - SLOTS).wait_send()

        make(j).start()

    def line(held, make, j, first, last):
        @pl.when((j >= 0) & (j < count))
        def _():
            at, slot = rows_of(j), slot_of(j)

            @pl.when(first)
            def _():
                held[slot, :] = own[at, :]

            @pl.when(jnp.logical_not(first))
            def _():
                make(j).wait_recv()
                held[slot, :] = held[slot, :] + own[at, :]

            @pl.when(jnp.logical_not(last))
            def _():
                send(make, j)

    settle = HOP * jnp.maximum(l, loops - 1 - l)
    lag = HOP * (loops - 1) + REACH * (longest + 1)
    starts = plan(parts, tiles, norbit, lag, count - 1 + HOP * (loops - 1), cuts + (tile_count - 1) * (cuts + 1))
    groups = len(starts)
    total_steps = max(count + lag, starts[-1] + 1)
    final = count - 2 * TILE * tiles // CHUNK

    def multiply(g, n):
        @pl.when(n == 0)
        def _():
            @pl.loop(0, tiles)
            def _(m):
                mine = pl.ds(pl.multiple_of(m * WIDE, WIDE), WIDE)
                for h in range(2):
                    block = 2 * g + h
                    high, low = split(own[row_of(block // blocks, m, lax.rem(block, blocks)), :].T)
                    left_ref[mine, h * TILE : (h + 1) * TILE] = high
                    left_ref[mine, SPAN + h * TILE : SPAN + (h + 1) * TILE] = high
                    left_ref[mine, 2 * SPAN + h * TILE : 2 * SPAN + (h + 1) * TILE] = low

        @pl.when(n > 0)
        def _():
            held, m = (n - 1) // tiles, lax.rem(n - 1, tiles)
            both = []
            for h in range(2):
                block = 2 * g + h
                both.append(cols[held, row_of(block // blocks, m, lax.rem(block, blocks)), :])
            high, low = split(jnp.concatenate(both, axis=0))
            right = jnp.concatenate([high, low, high], axis=0)
            theirs = pl.ds(pl.multiple_of((n - 1) * WIDE, WIDE), WIDE)

            @pl.when(g == 0)
            def _():
                acc_ref[:, theirs] = jnp.zeros((mrows, WIDE), jnp.float32)

            acc_ref[:, theirs] = acc_ref[:, theirs] + jnp.dot(left_ref[...], right, preferred_element_type=jnp.float32)

    def step(t, carry):
        line(pin, up, t - HOP * l, l == 0, l == loops - 1)
        line(sin, down, t - HOP * (loops - 1 - l), l == loops - 1, l == 0)

        done = t - settle

        @pl.when((done >= 0) & (done < count))
        def _():
            at, slot = rows_of(done), slot_of(done)
            total = pin[slot, :] + (sin[slot, :] - own[at, :])
            own[at, :] = total

            @pl.when(far == 0)
            def _():
                cols[core, at, :] = total

        passed = done - REACH * hops

        @pl.when((passed >= 0) & (passed < count))
        def _():
            @pl.when(far > 0)
            def _():
                chain(passed).wait_recv()

            @pl.when(forward)
            def _():
                send(chain, passed)

            @pl.when(backward)
            def _():
                send(back, passed)

            send(share, passed)

        ready = done - REACH * (longest + 1)

        @pl.when((ready >= 0) & (ready < count))
        def _():
            taken(ready).wait_recv()

        @pl.when((ready >= final) & (ready < count))
        def _():
            off = (ready - final) * CHUNK
            k = off // (tiles * TILE) * TILE + lax.rem(off, TILE)
            m = lax.rem(off // TILE, tiles)
            for held in range(2):
                high, low = split(cols[held, rows_of(ready), :])
                theirs = pl.ds(pl.multiple_of(held * mrows + m * WIDE, WIDE), WIDE)
                right_ref[pl.ds(pl.multiple_of(k, CHUNK), CHUNK), theirs] = high
                right_ref[pl.ds(pl.multiple_of(SPAN + k, CHUNK), CHUNK), theirs] = low

        g, begin = -1, 0
        for k, at in enumerate(starts):
            g = g + jnp.where(t >= at, 1, 0)
            begin = begin + jnp.where(t >= at, at - (starts[k - 1] if k else 0), 0)

        @pl.when((g >= 0) & (t - begin <= jnp.where(g < groups - 1, 2 * tiles, 0)))
        def _():
            multiply(g, t - begin)

        @pl.when(t < cuts)
        def _():
            prepare(t, 1)
            half(0, t, SPAN, norbit)

        later, q = 1 + (t - cuts) // (cuts + 1), lax.rem(t - cuts, cuts + 1)

        @pl.when((t >= cuts) & (later < tile_count) & (q < cuts))
        def _():
            half(later, q, 0, norbit)

        return carry

    lax.fori_loop(0, total_steps, step, 0)

    def drain(i, carry):
        j = count - SLOTS + i

        @pl.when(l < loops - 1)
        def _():
            up(j).wait_send()

        @pl.when(l > 0)
        def _():
            down(j).wait_send()

        @pl.when(forward)
        def _():
            chain(j).wait_send()

        @pl.when(backward)
        def _():
            back(j).wait_send()

        share(j).wait_send()
        return carry

    lax.fori_loop(0, SLOTS, drain, 0)


def finish_kernel(scale, acc_ref, left_ref, right_ref, out_ref):
    broad = out_ref.shape[1]
    at = pl.ds(pl.multiple_of(pl.program_id(0) * broad, broad), broad)
    right = jnp.concatenate([right_ref[:, at], right_ref[:SPAN, at]], axis=0)
    value = acc_ref[:, at] + jnp.dot(left_ref[...], right, preferred_element_type=jnp.float32)
    out_ref[...] = value * scale


def local(loops, row_count, integrals, mask, coeffs):
    nslab, naux, mrows, lcols = integrals.shape
    norbit = coeffs.shape[1]
    depth = nslab * naux * norbit
    tiles = mrows // WIDE
    count = depth * tiles * WIDE // (CHUNK * WIDE)
    assert lcols == 2 * mrows and row_count == 2 * loops and mrows % WIDE == 0
    assert norbit % TILE == 0 and norbit >= SPAN and depth % SPAN == 0
    deep = min(DEEP, lcols)
    cuts = lcols // deep
    buffers = min(BUFFERS, nslab * naux * tiles * cuts)
    assert cuts + 1 <= norbit // CHUNK and cuts <= min(buffers, SPAN // CHUNK) and norbit > SPAN
    spare = (8, 128) if 2 * norbit <= lcols and mrows % deep == 0 else (lcols, norbit)
    broad = min(BROAD, lcols)
    ring = min(count, max(SLOTS + 2 * HOP, HOP * (loops - 1)) + 2)
    lag, line = HOP * (loops - 1) + REACH * (row_count // 4 + 1), 2 * HOP + 6
    dma = pltpu.SemaphoreType.DMA
    vmem = pl.BlockSpec(memory_space=pltpu.VMEM)
    held = functools.partial(pltpu.with_memory_space_constraint, memory_space=pltpu.MemorySpace.HBM)
    partial = pl.pallas_call(
        functools.partial(exchange_kernel, loops, row_count),
        out_shape=[
            jax.ShapeDtypeStruct((mrows, lcols), jnp.float32),
            jax.ShapeDtypeStruct((mrows, 3 * SPAN), jnp.bfloat16),
            jax.ShapeDtypeStruct((2 * SPAN, lcols), jnp.bfloat16),
        ],
        in_specs=[
            pl.BlockSpec(memory_space=pl.ANY),
            pl.BlockSpec(memory_space=pl.ANY),
            pl.BlockSpec(memory_space=pl.ANY),
        ],
        out_specs=[vmem] * 3,
        scratch_shapes=[
            pltpu.VMEM((depth * tiles, WIDE), jnp.float32),
            pltpu.VMEM((ring * CHUNK, WIDE), jnp.float32),
            pltpu.VMEM((ring * CHUNK, WIDE), jnp.float32),
            pltpu.VMEM((2, depth * tiles, WIDE), jnp.float32),
            pltpu.VMEM((norbit, lcols), jnp.bfloat16),
            pltpu.VMEM((norbit, lcols), jnp.bfloat16),
            pltpu.VMEM((buffers, WIDE, deep), jnp.float32),
            pltpu.VMEM(spare, jnp.float32),
            dma((buffers,)),
            dma((2, cuts)),
        ]
        + [pltpu.SMEM(mask.shape, mask.dtype), dma]
        + [dma((min(count, slots),)) for slots in (SLOTS, line, SLOTS, line, SLOTS, 2 * lag + 4, SLOTS, lag + 10, SLOTS)],
        compiler_params=pltpu.CompilerParams(
            collective_id=0, has_side_effects=True, vmem_limit_bytes=42 << 20
        ),
        name="exchange",
    )(integrals, held(mask), held(coeffs))
    return pl.pallas_call(
        functools.partial(finish_kernel, float(depth) ** -0.5),
        grid=(lcols // broad,),
        out_shape=jax.ShapeDtypeStruct((mrows, lcols), jnp.float32),
        in_specs=[vmem] * 3,
        out_specs=pl.BlockSpec((mrows, broad), lambda n: (0, n)),
        compiler_params=pltpu.CompilerParams(vmem_limit_bytes=14 << 20),
        name="finish",
    )(*partial)


def solution(mesh):
    in_specs = (P(None, None, "rows", "loop"), P(None, "rows", "loop"), P("loop", None))
    out_specs = P("rows", "loop")
    body = functools.partial(local, mesh.shape["loop"], mesh.shape["rows"])
    return jax.shard_map(body, mesh=mesh, in_specs=in_specs, out_specs=out_specs, check_vma=False)
```

```python
import functools

import jax
import jax.numpy as jnp
from jax import lax
from jax.experimental import pallas as pl
from jax.experimental.pallas import tpu as pltpu
from jax.sharding import PartitionSpec as P

TILE = 128
WIDE = 2 * TILE
CHUNK = 64
SPAN = 256
DEEP = 512
HOP = 3
REACH = 3
SLOTS = 4
BUFFERS = 6
BROAD = 512
MESH = pl.DeviceIdType.MESH


def split(x):
    high = x.astype(jnp.bfloat16)
    low = (x - high.astype(jnp.float32)).astype(jnp.bfloat16)
    return high, low


def ring_place(pair, pairs):
    if pairs == 4:
        return pair + (pair // 2) * (1 - 2 * lax.rem(pair, 2))
    return pair


def place_of(part, tile, block, parts, tiles, norbit):
    inner = tile * norbit + block * TILE
    last = block * (tiles * TILE) + tile * TILE
    if isinstance(part, int):
        return part * tiles * norbit + (inner if part < parts - 1 else last)
    return part * (tiles * norbit) + jnp.where(part < parts - 1, inner, last)


def plan(parts, tiles, norbit, lag, last_done, free):
    groups, blocks = parts * norbit // SPAN, norbit // TILE
    starts = []
    for g in range(groups - 1):
        last = max(
            place_of(h // blocks, tiles - 1, h % blocks, parts, tiles, norbit) + TILE - 1 for h in (2 * g, 2 * g + 1)
        )
        starts.append(max(last // CHUNK + lag, free))
        free = starts[-1] + 1 + 2 * tiles
    return starts + [max(last_done, free)]


def exchange_kernel(
    loops, row_count, integrals_ref, mask_ref, coeffs_ref, acc_ref, left_ref, right_ref,
    own, pin, sin, cols, high_ref, low_ref, tile, spare, tile_sem, load_sem,
    keep_ref, keep_sem, up_send, up_recv, dn_send, dn_recv, ch_send, ch_recv, pt_send, pt_recv, bk_send,
):
    nslab, naux, mrows, lcols = integrals_ref.shape
    norbit = coeffs_ref.shape[1]
    parts = nslab * naux
    tiles = mrows // WIDE
    blocks = norbit // TILE
    tile_count = parts * tiles
    deep = tile.shape[2]
    cuts = lcols // deep
    buffers = tile.shape[0]
    count = own.shape[0] // CHUNK
    ring = pin.shape[0] // CHUNK
    pairs = row_count // 2
    r, l = lax.axis_index("rows"), lax.axis_index("loop")
    pair, core = r // 2, lax.rem(r, 2)
    partner = r + 1 - 2 * core
    turn = 1 - 2 * core
    place = ring_place(pair, pairs)
    far = lax.rem((place - ring_place(l, pairs)) * turn + pairs, pairs)
    ahead = ring_place(lax.rem(place + turn + pairs, pairs), pairs) * 2 + core
    behind = ring_place(lax.rem(place - turn + pairs, pairs), pairs) * 2 + core
    longest = pairs // 2
    hops = jnp.where(far <= longest, far, pairs - far)
    forward = far < longest
    backward = ((far == 0) & (longest < pairs - 1)) | (far > longest + 1)

    def deep_of(q):
        return pl.ds(pl.multiple_of(q * deep, deep), deep)

    def row_of(part, m, block):
        return pl.ds(pl.multiple_of(place_of(part, m, block, parts, tiles, norbit), TILE), TILE)

    def fetch(u, q):
        part, m = u // tiles, lax.rem(u, tiles)
        slot = lax.rem(u * cuts + q, buffers)
        return pltpu.make_async_copy(
            integrals_ref.at[
                part // naux, lax.rem(part, naux), pl.ds(pl.multiple_of(m * WIDE, WIDE), WIDE), deep_of(q)
            ],
            tile.at[slot],
            tile_sem.at[slot],
        )

    def fetch_next(u, q):
        i = u * cuts + q + buffers

        @pl.when(i < tile_count * cuts)
        def _():
            fetch(i // cuts, lax.rem(i, cuts)).start()

    ranges = ((0, SPAN), (SPAN, norbit))

    def landing(q, k):
        low, high = ranges[k]
        if spare.shape == coeffs_ref.shape:
            return spare.at[deep_of(q), low:high]
        first, rows = q * deep // mrows, lax.rem(q * deep, mrows)
        at = pl.ds(pl.multiple_of(first * norbit + low, TILE), high - low)
        return acc_ref.at[pl.ds(pl.multiple_of(rows, deep), deep), at]

    def load(q, k):
        return pltpu.make_async_copy(
            coeffs_ref.at[deep_of(q), ranges[k][0] : ranges[k][1]], landing(q, k), load_sem.at[k, q]
        )

    def prepare(q, k):
        load(q, k).wait()
        rows = slice(*ranges[k])
        held = landing(q, k)
        for n in range(deep // 256):
            at = pl.ds(pl.multiple_of(q * deep + n * 256, 256), 256)
            high_ref[rows, at], low_ref[rows, at] = split(held[n * 256 : (n + 1) * 256, :].T)

    def half(u, q, first, last):
        part, m = u // tiles, lax.rem(u, tiles)
        slab = part // naux
        own_blocks = range(first // TILE, last // TILE)
        if first == 0:
            fetch(u, q).wait()

        @pl.when(q == 0)
        def _():
            for b in own_blocks:
                own[row_of(part, m, b), :] = jnp.zeros((TILE, WIDE), jnp.float32)

        def piece(i, j):
            keep = keep_ref[slab, m * (WIDE // TILE) + i, q * (deep // TILE) + j].astype(jnp.float32)
            return tile[lax.rem(u * cuts + q, buffers), i * TILE : (i + 1) * TILE, j * TILE : (j + 1) * TILE] * keep

        held = jnp.concatenate(
            [jnp.concatenate([piece(i, j) for j in range(deep // TILE)], axis=1) for i in range(WIDE // TILE)], axis=0
        )
        high, low = split(held)

        def times(a, b):
            return lax.dot_general(a, b, (((1,), (1,)), ((), ())), preferred_element_type=jnp.float32)

        at = deep_of(q)
        upper, lower = high_ref[first:last, at], low_ref[first:last, at]
        value = times(upper, high) + times(upper, low) + times(lower, high)
        for b in own_blocks:
            rows = row_of(part, m, b)
            own[rows, :] = own[rows, :] + value[b * TILE - first : (b + 1) * TILE - first]

        if last == norbit:
            fetch_next(u, q)

    taken_mask = pltpu.make_async_copy(mask_ref, keep_ref, keep_sem)
    taken_mask.start()
    for q in range(cuts):
        load(q, 0).start()
        fetch(0, q).start()
    for q in range(cuts):
        load(q, 1).start()
    for i in range(cuts, buffers):
        fetch(i // cuts, i % cuts).start()

    barrier = pltpu.get_barrier_semaphore()
    for other in (partner, ahead, behind):
        pl.semaphore_signal(barrier, inc=1, device_id={"rows": other}, device_id_type=MESH)

    @pl.when(l > 0)
    def _():
        pl.semaphore_signal(barrier, inc=1, device_id={"loop": l - 1}, device_id_type=MESH)

    @pl.when(l < loops - 1)
    def _():
        pl.semaphore_signal(barrier, inc=1, device_id={"loop": l + 1}, device_id_type=MESH)

    taken_mask.wait()

    @pl.loop(0, cuts)
    def _(q):
        prepare(q, 0)
        half(0, q, 0, SPAN)

    neighbours = jnp.where(l > 0, 1, 0) + jnp.where(l < loops - 1, 1, 0)
    pl.semaphore_wait(barrier, 3 + neighbours)

    def rows_of(j):
        return pl.ds(pl.multiple_of(j * CHUNK, CHUNK), CHUNK)

    def slot_of(j):
        return pl.ds(pl.multiple_of(lax.rem(j, ring) * CHUNK, CHUNK), CHUNK)

    def copy(src, dst, send, recv, j, target):
        return pltpu.make_async_remote_copy(
            src_ref=src, dst_ref=dst, send_sem=send.at[lax.rem(j, SLOTS)], recv_sem=recv.at[lax.rem(j, recv.shape[0])],
            device_id=target, device_id_type=MESH,
        )

    def up(j):
        return copy(pin.at[slot_of(j)], pin.at[slot_of(j)], up_send, up_recv, j, {"loop": l + 1})

    def down(j):
        return copy(sin.at[slot_of(j)], sin.at[slot_of(j)], dn_send, dn_recv, j, {"loop": l - 1})

    def chain(j):
        ref = cols.at[core, rows_of(j)]
        return copy(ref, ref, ch_send, ch_recv, j, {"rows": ahead})

    def back(j):
        ref = cols.at[core, rows_of(j)]
        return copy(ref, ref, bk_send, ch_recv, j, {"rows": behind})

    def share(j):
        ref = cols.at[core, rows_of(j)]
        return copy(ref, ref, pt_send, pt_recv, j, {"rows": partner})

    def taken(j):
        ref = cols.at[1 - core, rows_of(j)]
        return copy(ref, ref, pt_send, pt_recv, j, {"rows": partner})

    def send(make, j):
        @pl.when(j >= SLOTS)
        def _():
            make(j - SLOTS).wait_send()

        make(j).start()

    def line(held, make, j, first, last):
        @pl.when((j >= 0) & (j < count))
        def _():
            at, slot = rows_of(j), slot_of(j)

            @pl.when(first)
            def _():
                held[slot, :] = own[at, :]

            @pl.when(jnp.logical_not(first))
            def _():
                make(j).wait_recv()
                held[slot, :] = held[slot, :] + own[at, :]

            @pl.when(jnp.logical_not(last))
            def _():
                send(make, j)

    settle = HOP * jnp.maximum(l, loops - 1 - l)
    lag = HOP * (loops - 1) + REACH * (longest + 1)
    halves = cuts + (tile_count - 1) * (cuts + 1) + HOP * ((loops - 1) // 2)
    starts = plan(parts, tiles, norbit, lag, count - 1 + HOP * (loops - 1), halves)
    groups = len(starts)
    total_steps = max(count + lag, starts[-1] + 1)
    final = count - 2 * TILE * tiles // CHUNK

    def multiply(g, n):
        @pl.when(n == 0)
        def _():
            @pl.loop(0, tiles)
            def _(m):
                mine = pl.ds(pl.multiple_of(m * WIDE, WIDE), WIDE)
                for h in range(2):
                    block = 2 * g + h
                    high, low = split(own[row_of(block // blocks, m, lax.rem(block, blocks)), :].T)
                    left_ref[mine, h * TILE : (h + 1) * TILE] = high
                    left_ref[mine, SPAN + h * TILE : SPAN + (h + 1) * TILE] = high
                    left_ref[mine, 2 * SPAN + h * TILE : 2 * SPAN + (h + 1) * TILE] = low

        @pl.when(n > 0)
        def _():
            held, m = (n - 1) // tiles, lax.rem(n - 1, tiles)
            both = []
            for h in range(2):
                block = 2 * g + h
                both.append(cols[held, row_of(block // blocks, m, lax.rem(block, blocks)), :])
            high, low = split(jnp.concatenate(both, axis=0))
            right = jnp.concatenate([high, low, high], axis=0)
            theirs = pl.ds(pl.multiple_of((n - 1) * WIDE, WIDE), WIDE)

            @pl.when(g == 0)
            def _():
                acc_ref[:, theirs] = jnp.zeros((mrows, WIDE), jnp.float32)

            acc_ref[:, theirs] = acc_ref[:, theirs] + jnp.dot(left_ref[...], right, preferred_element_type=jnp.float32)

    def step(t, carry):
        line(pin, up, t - HOP * l, l == 0, l == loops - 1)
        line(sin, down, t - HOP * (loops - 1 - l), l == loops - 1, l == 0)

        done = t - settle

        @pl.when((done >= 0) & (done < count))
        def _():
            at, slot = rows_of(done), slot_of(done)
            total = pin[slot, :] + (sin[slot, :] - own[at, :])
            own[at, :] = total

            @pl.when(far == 0)
            def _():
                cols[core, at, :] = total

        passed = done - REACH * hops

        @pl.when((passed >= 0) & (passed < count))
        def _():
            @pl.when(far > 0)
            def _():
                chain(passed).wait_recv()

            @pl.when(forward)
            def _():
                send(chain, passed)

            @pl.when(backward)
            def _():
                send(back, passed)

            send(share, passed)

        ready = done - REACH * (longest + 1)

        @pl.when((ready >= 0) & (ready < count))
        def _():
            taken(ready).wait_recv()

        @pl.when((ready >= final) & (ready < count))
        def _():
            off = (ready - final) * CHUNK
            k = off // (tiles * TILE) * TILE + lax.rem(off, TILE)
            m = lax.rem(off // TILE, tiles)
            for held in range(2):
                high, low = split(cols[held, rows_of(ready), :])
                theirs = pl.ds(pl.multiple_of(held * mrows + m * WIDE, WIDE), WIDE)
                right_ref[pl.ds(pl.multiple_of(k, CHUNK), CHUNK), theirs] = high
                right_ref[pl.ds(pl.multiple_of(SPAN + k, CHUNK), CHUNK), theirs] = low

        g, begin = -1, 0
        for k, at in enumerate(starts):
            g = g + jnp.where(t >= at, 1, 0)
            begin = begin + jnp.where(t >= at, at - (starts[k - 1] if k else 0), 0)

        @pl.when((g >= 0) & (t - begin <= jnp.where(g < groups - 1, 2 * tiles, 0)))
        def _():
            multiply(g, t - begin)

        since = t - HOP * jnp.minimum(l, loops - 1 - l)

        @pl.when((since >= 0) & (since < cuts))
        def _():
            prepare(since, 1)
            half(0, since, SPAN, norbit)

        past = since - cuts
        later, q = 1 + past // (cuts + 1), lax.rem(past, cuts + 1)

        @pl.when((past >= 0) & (later < tile_count) & (q < cuts))
        def _():
            half(later, q, 0, norbit)

        return carry

    lax.fori_loop(0, total_steps, step, 0)

    def drain(i, carry):
        j = count - SLOTS + i

        @pl.when(l < loops - 1)
        def _():
            up(j).wait_send()

        @pl.when(l > 0)
        def _():
            down(j).wait_send()

        @pl.when(forward)
        def _():
            chain(j).wait_send()

        @pl.when(backward)
        def _():
            back(j).wait_send()

        share(j).wait_send()
        return carry

    lax.fori_loop(0, SLOTS, drain, 0)


def finish_kernel(scale, acc_ref, left_ref, right_ref, out_ref):
    broad = out_ref.shape[1]
    at = pl.ds(pl.multiple_of(pl.program_id(0) * broad, broad), broad)
    right = jnp.concatenate([right_ref[:, at], right_ref[:SPAN, at]], axis=0)
    value = acc_ref[:, at] + jnp.dot(left_ref[...], right, preferred_element_type=jnp.float32)
    out_ref[...] = value * scale


def local(loops, row_count, integrals, mask, coeffs):
    nslab, naux, mrows, lcols = integrals.shape
    norbit = coeffs.shape[1]
    depth = nslab * naux * norbit
    tiles = mrows // WIDE
    count = depth * tiles * WIDE // (CHUNK * WIDE)
    assert lcols == 2 * mrows and row_count == 2 * loops and mrows % WIDE == 0
    assert norbit % TILE == 0 and norbit >= SPAN and depth % SPAN == 0
    deep = min(DEEP, lcols)
    cuts = lcols // deep
    buffers = min(BUFFERS, nslab * naux * tiles * cuts)
    assert cuts + 1 <= norbit // CHUNK and cuts <= min(buffers, SPAN // CHUNK) and norbit > SPAN
    spare = (8, 128) if 2 * norbit <= lcols and mrows % deep == 0 else (lcols, norbit)
    broad = min(BROAD, lcols)
    ring = min(count, max(SLOTS + 2 * HOP, HOP * (loops - 1)) + 6)
    lag, line = HOP * (loops - 1) + REACH * (row_count // 4 + 1), HOP * loops
    dma = pltpu.SemaphoreType.DMA
    vmem = pl.BlockSpec(memory_space=pltpu.VMEM)
    held = functools.partial(pltpu.with_memory_space_constraint, memory_space=pltpu.MemorySpace.HBM)
    partial = pl.pallas_call(
        functools.partial(exchange_kernel, loops, row_count),
        out_shape=[
            jax.ShapeDtypeStruct((mrows, lcols), jnp.float32),
            jax.ShapeDtypeStruct((mrows, 3 * SPAN), jnp.bfloat16),
            jax.ShapeDtypeStruct((2 * SPAN, lcols), jnp.bfloat16),
        ],
        in_specs=[
            pl.BlockSpec(memory_space=pl.ANY),
            pl.BlockSpec(memory_space=pl.ANY),
            pl.BlockSpec(memory_space=pl.ANY),
        ],
        out_specs=[vmem] * 3,
        scratch_shapes=[
            pltpu.VMEM((depth * tiles, WIDE), jnp.float32),
            pltpu.VMEM((ring * CHUNK, WIDE), jnp.float32),
            pltpu.VMEM((ring * CHUNK, WIDE), jnp.float32),
            pltpu.VMEM((2, depth * tiles, WIDE), jnp.float32),
            pltpu.VMEM((norbit, lcols), jnp.bfloat16),
            pltpu.VMEM((norbit, lcols), jnp.bfloat16),
            pltpu.VMEM((buffers, WIDE, deep), jnp.float32),
            pltpu.VMEM(spare, jnp.float32),
            dma((buffers,)),
            dma((2, cuts)),
        ]
        + [pltpu.SMEM(mask.shape, mask.dtype), dma]
        + [dma((min(count, slots),)) for slots in (SLOTS, line, SLOTS, line, SLOTS, 2 * lag, SLOTS, lag + 8, SLOTS)],
        compiler_params=pltpu.CompilerParams(
            collective_id=0, has_side_effects=True, vmem_limit_bytes=42 << 20
        ),
        name="exchange",
    )(integrals, held(mask), held(coeffs))
    return pl.pallas_call(
        functools.partial(finish_kernel, float(depth) ** -0.5),
        grid=(lcols // broad,),
        out_shape=jax.ShapeDtypeStruct((mrows, lcols), jnp.float32),
        in_specs=[vmem] * 3,
        out_specs=pl.BlockSpec((mrows, broad), lambda n: (0, n)),
        compiler_params=pltpu.CompilerParams(vmem_limit_bytes=14 << 20),
        name="finish",
    )(*partial)


def solution(mesh):
    in_specs = (P(None, None, "rows", "loop"), P(None, "rows", "loop"), P("loop", None))
    out_specs = P("rows", "loop")
    body = functools.partial(local, mesh.shape["loop"], mesh.shape["rows"])
    return jax.shard_map(body, mesh=mesh, in_specs=in_specs, out_specs=out_specs, check_vma=False)
```

```python
import functools

import jax
import jax.numpy as jnp
from jax import lax
from jax.experimental import pallas as pl
from jax.experimental.pallas import tpu as pltpu
from jax.sharding import PartitionSpec as P

TILE = 128
WIDE = 2 * TILE
CHUNK = 64
SPAN = 256
DEEP = 512
HOP = 3
REACH = 3
SLOTS = 4
BUFFERS = 6
BROAD = 512
MESH = pl.DeviceIdType.MESH


def split(x):
    high = x.astype(jnp.bfloat16)
    low = (x - high.astype(jnp.float32)).astype(jnp.bfloat16)
    return high, low


def ring_place(pair, pairs):
    if pairs == 4:
        return pair + (pair // 2) * (1 - 2 * lax.rem(pair, 2))
    return pair


def place_of(part, tile, block, parts, tiles, norbit):
    inner = tile * norbit + block * TILE
    last = block * (tiles * TILE) + tile * TILE
    if isinstance(part, int):
        return part * tiles * norbit + (inner if part < parts - 1 else last)
    return part * (tiles * norbit) + jnp.where(part < parts - 1, inner, last)


def plan(parts, tiles, norbit, lag, last_done, free):
    groups, blocks = parts * norbit // SPAN, norbit // TILE
    starts = []
    for g in range(groups - 1):
        last = max(
            place_of(h // blocks, tiles - 1, h % blocks, parts, tiles, norbit) + TILE - 1 for h in (2 * g, 2 * g + 1)
        )
        starts.append(max(last // CHUNK + lag, free))
        free = starts[-1] + 1 + 2 * tiles
    return starts + [max(last_done, free)]


def exchange_kernel(
    loops, row_count, integrals_ref, mask_ref, coeffs_ref, acc_ref, left_ref, right_ref,
    own, pin, sin, cols, high_ref, low_ref, tile, spare, tile_sem, load_sem,
    keep_ref, keep_sem, up_send, up_recv, dn_send, dn_recv, ch_send, ch_recv, pt_send, pt_recv, bk_send,
):
    nslab, naux, mrows, lcols = integrals_ref.shape
    norbit = coeffs_ref.shape[1]
    parts = nslab * naux
    tiles = mrows // WIDE
    blocks = norbit // TILE
    tile_count = parts * tiles
    deep = tile.shape[2]
    cuts = lcols // deep
    buffers = tile.shape[0]
    count = own.shape[0] // CHUNK
    ring = pin.shape[0] // CHUNK
    pairs = row_count // 2
    r, l = lax.axis_index("rows"), lax.axis_index("loop")
    pair, core = r // 2, lax.rem(r, 2)
    partner = r + 1 - 2 * core
    turn = 1 - 2 * core
    place = ring_place(pair, pairs)
    far = lax.rem((place - ring_place(l, pairs)) * turn + pairs, pairs)
    ahead = ring_place(lax.rem(place + turn + pairs, pairs), pairs) * 2 + core
    behind = ring_place(lax.rem(place - turn + pairs, pairs), pairs) * 2 + core
    longest = pairs // 2
    hops = jnp.where(far <= longest, far, pairs - far)
    forward = far < longest
    backward = ((far == 0) & (longest < pairs - 1)) | (far > longest + 1)

    def deep_of(q):
        return pl.ds(pl.multiple_of(q * deep, deep), deep)

    def row_of(part, m, block):
        return pl.ds(pl.multiple_of(place_of(part, m, block, parts, tiles, norbit), TILE), TILE)

    def fetch(u, q):
        part, m = u // tiles, lax.rem(u, tiles)
        slot = lax.rem(u * cuts + q, buffers)
        return pltpu.make_async_copy(
            integrals_ref.at[
                part // naux, lax.rem(part, naux), pl.ds(pl.multiple_of(m * WIDE, WIDE), WIDE), deep_of(q)
            ],
            tile.at[slot],
            tile_sem.at[slot],
        )

    def fetch_next(u, q):
        i = u * cuts + q + buffers

        @pl.when(i < tile_count * cuts)
        def _():
            fetch(i // cuts, lax.rem(i, cuts)).start()

    ranges = ((0, SPAN), (SPAN, norbit))

    def landing(q, k):
        low, high = ranges[k]
        if spare.shape == coeffs_ref.shape:
            return spare.at[deep_of(q), low:high]
        first, rows = q * deep // mrows, lax.rem(q * deep, mrows)
        at = pl.ds(pl.multiple_of(first * norbit + low, TILE), high - low)
        return acc_ref.at[pl.ds(pl.multiple_of(rows, deep), deep), at]

    def load(q, k):
        return pltpu.make_async_copy(
            coeffs_ref.at[deep_of(q), ranges[k][0] : ranges[k][1]], landing(q, k), load_sem.at[k, q]
        )

    def prepare(q, k):
        load(q, k).wait()
        rows = slice(*ranges[k])
        held = landing(q, k)
        for n in range(deep // 256):
            at = pl.ds(pl.multiple_of(q * deep + n * 256, 256), 256)
            high_ref[rows, at], low_ref[rows, at] = split(held[n * 256 : (n + 1) * 256, :].T)

    def half(u, q, first, last):
        part, m = u // tiles, lax.rem(u, tiles)
        slab = part // naux
        own_blocks = range(first // TILE, last // TILE)
        if first == 0:
            fetch(u, q).wait()

        @pl.when(q == 0)
        def _():
            for b in own_blocks:
                own[row_of(part, m, b), :] = jnp.zeros((TILE, WIDE), jnp.float32)

        def piece(i, j):
            keep = keep_ref[slab, m * (WIDE // TILE) + i, q * (deep // TILE) + j].astype(jnp.float32)
            return tile[lax.rem(u * cuts + q, buffers), i * TILE : (i + 1) * TILE, j * TILE : (j + 1) * TILE] * keep

        held = jnp.concatenate(
            [jnp.concatenate([piece(i, j) for j in range(deep // TILE)], axis=1) for i in range(WIDE // TILE)], axis=0
        )
        high, low = split(held)

        def times(a, b):
            return lax.dot_general(a, b, (((1,), (1,)), ((), ())), preferred_element_type=jnp.float32)

        at = deep_of(q)
        upper, lower = high_ref[first:last, at], low_ref[first:last, at]
        value = times(upper, high) + times(upper, low) + times(lower, high)
        for b in own_blocks:
            rows = row_of(part, m, b)
            own[rows, :] = own[rows, :] + value[b * TILE - first : (b + 1) * TILE - first]

        if last == norbit:
            fetch_next(u, q)

    taken_mask = pltpu.make_async_copy(mask_ref, keep_ref, keep_sem)
    taken_mask.start()
    for q in range(cuts):
        load(q, 0).start()
        fetch(0, q).start()
    for q in range(cuts):
        load(q, 1).start()
    for i in range(cuts, buffers):
        fetch(i // cuts, i % cuts).start()

    barrier = pltpu.get_barrier_semaphore()
    for other in (partner, ahead, behind):
        pl.semaphore_signal(barrier, inc=1, device_id={"rows": other}, device_id_type=MESH)

    @pl.when(l > 0)
    def _():
        pl.semaphore_signal(barrier, inc=1, device_id={"loop": l - 1}, device_id_type=MESH)

    @pl.when(l < loops - 1)
    def _():
        pl.semaphore_signal(barrier, inc=1, device_id={"loop": l + 1}, device_id_type=MESH)

    taken_mask.wait()

    @pl.loop(0, cuts)
    def _(q):
        prepare(q, 0)
        half(0, q, 0, SPAN)

    neighbours = jnp.where(l > 0, 1, 0) + jnp.where(l < loops - 1, 1, 0)
    pl.semaphore_wait(barrier, 3 + neighbours)

    def rows_of(j):
        return pl.ds(pl.multiple_of(j * CHUNK, CHUNK), CHUNK)

    def slot_of(j):
        return pl.ds(pl.multiple_of(lax.rem(j, ring) * CHUNK, CHUNK), CHUNK)

    def copy(src, dst, send, recv, j, target):
        return pltpu.make_async_remote_copy(
            src_ref=src, dst_ref=dst, send_sem=send.at[lax.rem(j, SLOTS)], recv_sem=recv.at[lax.rem(j, recv.shape[0])],
            device_id=target, device_id_type=MESH,
        )

    def up(j):
        return copy(pin.at[slot_of(j)], pin.at[slot_of(j)], up_send, up_recv, j, {"loop": l + 1})

    def down(j):
        return copy(sin.at[slot_of(j)], sin.at[slot_of(j)], dn_send, dn_recv, j, {"loop": l - 1})

    def chain(j):
        ref = cols.at[core, rows_of(j)]
        return copy(ref, ref, ch_send, ch_recv, j, {"rows": ahead})

    def back(j):
        ref = cols.at[core, rows_of(j)]
        return copy(ref, ref, bk_send, ch_recv, j, {"rows": behind})

    def share(j):
        ref = cols.at[core, rows_of(j)]
        return copy(ref, ref, pt_send, pt_recv, j, {"rows": partner})

    def taken(j):
        ref = cols.at[1 - core, rows_of(j)]
        return copy(ref, ref, pt_send, pt_recv, j, {"rows": partner})

    def send(make, j):
        @pl.when(j >= SLOTS)
        def _():
            make(j - SLOTS).wait_send()

        make(j).start()

    def line(held, make, j, first, last):
        @pl.when((j >= 0) & (j < count))
        def _():
            at, slot = rows_of(j), slot_of(j)

            @pl.when(first)
            def _():
                held[slot, :] = own[at, :]

            @pl.when(jnp.logical_not(first))
            def _():
                make(j).wait_recv()
                held[slot, :] = held[slot, :] + own[at, :]

            @pl.when(jnp.logical_not(last))
            def _():
                send(make, j)

    settle = HOP * jnp.maximum(l, loops - 1 - l)
    lag = HOP * (loops - 1) + REACH * (longest + 1)
    halves = cuts + (tile_count - 1) * (cuts + 1) + HOP * ((loops - 1) // 2)
    starts = plan(parts, tiles, norbit, lag, count - 1 + HOP * (loops - 1), halves)
    groups = len(starts)
    total_steps = max(count + lag, starts[-1] + 1)
    final = count - 2 * TILE * tiles // CHUNK

    def multiply(g, n):
        @pl.when(n == 0)
        def _():
            @pl.loop(0, tiles)
            def _(m):
                mine = pl.ds(pl.multiple_of(m * WIDE, WIDE), WIDE)
                for h in range(2):
                    block = 2 * g + h
                    high, low = split(own[row_of(block // blocks, m, lax.rem(block, blocks)), :].T)
                    left_ref[mine, h * TILE : (h + 1) * TILE] = high
                    left_ref[mine, SPAN + h * TILE : SPAN + (h + 1) * TILE] = high
                    left_ref[mine, 2 * SPAN + h * TILE : 2 * SPAN + (h + 1) * TILE] = low

        @pl.when(n > 0)
        def _():
            held, m = (n - 1) // tiles, lax.rem(n - 1, tiles)
            both = []
            for h in range(2):
                block = 2 * g + h
                both.append(cols[held, row_of(block // blocks, m, lax.rem(block, blocks)), :])
            high, low = split(jnp.concatenate(both, axis=0))
            right = jnp.concatenate([high, low, high], axis=0)
            theirs = pl.ds(pl.multiple_of((n - 1) * WIDE, WIDE), WIDE)

            @pl.when(g == 0)
            def _():
                acc_ref[:, theirs] = jnp.zeros((mrows, WIDE), jnp.float32)

            acc_ref[:, theirs] = acc_ref[:, theirs] + jnp.dot(left_ref[...], right, preferred_element_type=jnp.float32)

    def step(t, carry):
        line(pin, up, t - HOP * l, l == 0, l == loops - 1)
        line(sin, down, t - HOP * (loops - 1 - l), l == loops - 1, l == 0)

        done = t - settle

        @pl.when((done >= 0) & (done < count))
        def _():
            at, slot = rows_of(done), slot_of(done)
            total = pin[slot, :] + (sin[slot, :] - own[at, :])
            own[at, :] = total

            @pl.when(far == 0)
            def _():
                cols[core, at, :] = total

        passed = done - REACH * hops

        @pl.when((passed >= 0) & (passed < count))
        def _():
            @pl.when(far > 0)
            def _():
                chain(passed).wait_recv()

            @pl.when(forward)
            def _():
                send(chain, passed)

            @pl.when(backward)
            def _():
                send(back, passed)

            send(share, passed)

        ready = done - REACH * (longest + 1)

        @pl.when((ready >= 0) & (ready < count))
        def _():
            taken(ready).wait_recv()

        @pl.when((ready >= final) & (ready < count))
        def _():
            off = (ready - final) * CHUNK
            k = off // (tiles * TILE) * TILE + lax.rem(off, TILE)
            m = lax.rem(off // TILE, tiles)
            for held in range(2):
                high, low = split(cols[held, rows_of(ready), :])
                theirs = pl.ds(pl.multiple_of(held * mrows + m * WIDE, WIDE), WIDE)
                right_ref[pl.ds(pl.multiple_of(k, CHUNK), CHUNK), theirs] = high
                right_ref[pl.ds(pl.multiple_of(SPAN + k, CHUNK), CHUNK), theirs] = low

        g, begin = -1, 0
        for k, at in enumerate(starts):
            g = g + jnp.where(t >= at, 1, 0)
            begin = begin + jnp.where(t >= at, at - (starts[k - 1] if k else 0), 0)

        @pl.when((g >= 0) & (t - begin <= jnp.where(g < groups - 1, 2 * tiles, 0)))
        def _():
            multiply(g, t - begin)

        since = t - HOP * jnp.minimum(l, loops - 1 - l)

        @pl.when((since >= 0) & (since < cuts))
        def _():
            prepare(since, 1)
            half(0, since, SPAN, norbit)

        past = since - cuts
        later, q = 1 + past // (cuts + 1), lax.rem(past, cuts + 1)

        @pl.when((past >= 0) & (later < tile_count) & (q < cuts))
        def _():
            half(later, q, 0, norbit)

        return carry

    lax.fori_loop(0, total_steps, step, 0)

    def drain(i, carry):
        j = count - SLOTS + i

        @pl.when(l < loops - 1)
        def _():
            up(j).wait_send()

        @pl.when(l > 0)
        def _():
            down(j).wait_send()

        @pl.when(forward)
        def _():
            chain(j).wait_send()

        @pl.when(backward)
        def _():
            back(j).wait_send()

        share(j).wait_send()
        return carry

    lax.fori_loop(0, SLOTS, drain, 0)


def finish_kernel(scale, acc_ref, left_ref, right_ref, out_ref):
    broad = out_ref.shape[1]
    at = pl.ds(pl.multiple_of(pl.program_id(0) * broad, broad), broad)
    both, deep = left_ref[:, : 2 * SPAN], left_ref[:, 2 * SPAN :]
    value = jnp.dot(both, right_ref[:, at], preferred_element_type=jnp.float32)
    value = value + jnp.dot(deep, right_ref[:SPAN, at], preferred_element_type=jnp.float32)
    out_ref[...] = (acc_ref[:, at] + value) * scale


def local(loops, row_count, integrals, mask, coeffs):
    nslab, naux, mrows, lcols = integrals.shape
    norbit = coeffs.shape[1]
    depth = nslab * naux * norbit
    tiles = mrows // WIDE
    count = depth * tiles * WIDE // (CHUNK * WIDE)
    assert lcols == 2 * mrows and row_count == 2 * loops and mrows % WIDE == 0
    assert norbit % TILE == 0 and norbit >= SPAN and depth % SPAN == 0
    deep = min(DEEP, lcols)
    cuts = lcols // deep
    buffers = min(BUFFERS, nslab * naux * tiles * cuts)
    assert cuts + 1 <= norbit // CHUNK and cuts <= min(buffers, SPAN // CHUNK) and norbit > SPAN
    spare = (8, 128) if 2 * norbit <= lcols and mrows % deep == 0 else (lcols, norbit)
    broad = min(BROAD, lcols)
    ring = min(count, max(SLOTS + 2 * HOP, HOP * (loops - 1)) + 6)
    lag, line = HOP * (loops - 1) + REACH * (row_count // 4 + 1), HOP * loops
    dma = pltpu.SemaphoreType.DMA
    vmem = pl.BlockSpec(memory_space=pltpu.VMEM)
    held = functools.partial(pltpu.with_memory_space_constraint, memory_space=pltpu.MemorySpace.HBM)
    partial = pl.pallas_call(
        functools.partial(exchange_kernel, loops, row_count),
        out_shape=[
            jax.ShapeDtypeStruct((mrows, lcols), jnp.float32),
            jax.ShapeDtypeStruct((mrows, 3 * SPAN), jnp.bfloat16),
            jax.ShapeDtypeStruct((2 * SPAN, lcols), jnp.bfloat16),
        ],
        in_specs=[
            pl.BlockSpec(memory_space=pl.ANY),
            pl.BlockSpec(memory_space=pl.ANY),
            pl.BlockSpec(memory_space=pl.ANY),
        ],
        out_specs=[vmem] * 3,
        scratch_shapes=[
            pltpu.VMEM((depth * tiles, WIDE), jnp.float32),
            pltpu.VMEM((ring * CHUNK, WIDE), jnp.float32),
            pltpu.VMEM((ring * CHUNK, WIDE), jnp.float32),
            pltpu.VMEM((2, depth * tiles, WIDE), jnp.float32),
            pltpu.VMEM((norbit, lcols), jnp.bfloat16),
            pltpu.VMEM((norbit, lcols), jnp.bfloat16),
            pltpu.VMEM((buffers, WIDE, deep), jnp.float32),
            pltpu.VMEM(spare, jnp.float32),
            dma((buffers,)),
            dma((2, cuts)),
        ]
        + [pltpu.SMEM(mask.shape, mask.dtype), dma]
        + [dma((min(count, slots),)) for slots in (SLOTS, line, SLOTS, line, SLOTS, 2 * lag, SLOTS, lag + 8, SLOTS)],
        compiler_params=pltpu.CompilerParams(
            collective_id=0, has_side_effects=True, vmem_limit_bytes=42 << 20
        ),
        name="exchange",
    )(integrals, held(mask), held(coeffs))
    return pl.pallas_call(
        functools.partial(finish_kernel, float(depth) ** -0.5),
        grid=(lcols // broad,),
        out_shape=jax.ShapeDtypeStruct((mrows, lcols), jnp.float32),
        in_specs=[vmem] * 3,
        out_specs=pl.BlockSpec((mrows, broad), lambda n: (0, n)),
        compiler_params=pltpu.CompilerParams(vmem_limit_bytes=14 << 20),
        name="finish",
    )(*partial)


def solution(mesh):
    in_specs = (P(None, None, "rows", "loop"), P(None, "rows", "loop"), P("loop", None))
    out_specs = P("rows", "loop")
    body = functools.partial(local, mesh.shape["loop"], mesh.shape["rows"])
    return jax.shard_map(body, mesh=mesh, in_specs=in_specs, out_specs=out_specs, check_vma=False)
```
